256 devices in a mesh: lat: 32 (over y, z_lo, x), lev: 8 (over z_hi, core).
Axes of the slice: x: 4, y: 4, z: 8 (z_hi: 4, z_lo: 2; z = z_hi * 2 + z_lo), core: 2. Of those that a mesh axis runs over, the one named last changes fastest.
Arguments:
- prognostic: float32 [4, 24, 256, 768], P(None, 'lev', 'lat'), may hold values from -6 to 6
- cotangent: bfloat16 [4, 24, 256, 768], P(None, 'lev', 'lat'), may hold values from -6 to 6
- damping: float32 [4, 24], P(None, 'lev'), may hold values from 1 to 30
- in_scale: float32 [4, 24], replicated, may hold values from 0.5 to 4
- w_in: bfloat16 [512, 96], replicated, may hold values from -0.625 to 0.625
- b_in: float32 [512], replicated, may hold values from -3 to 3
- w_mid: bfloat16 [512, 512], replicated, may hold values from -0.25 to 0.25
- b_mid: float32 [512], replicated, may hold values from -3 to 3
- w_out: bfloat16 [96, 512], replicated, may hold values from -0.25 to 0.25
- wave_order: int32 [256], replicated, may hold values from 0 to 255, as said below
- lat_order: int32 [256], replicated, may hold values from 0 to 255, each once
Outputs:
- new_state: float32 [4, 24, 256, 768], P(None, 'lev', 'lat')
- spectral: float32 [256, 2, 4, 24, 256], P('lat', None, None, 'lev')
- grad_w_in: float32 [512, 96], replicated
- grad_b_in: float32 [512], replicated
- grad_w_mid: float32 [512, 512], replicated
- grad_b_mid: float32 [512], replicated
- grad_w_out: float32 [96, 512], replicated
The draws below stay inside these ranges and needn't reach their ends.
Inputs may be any that keep to these rules, and one draw needn't show every extreme that they name: `wave_order`: A permutation of the wavenumbers. Block d, entries d * 8 to (d + 1) * 8 - 1, lists the wavenumbers owned by index d of lat: one from each run of 32 consecutive wavenumbers, taken from alternate ends of the runs so that the triangular work of the blocks is nearly equal. `lat_order`: A permutation of the latitudes.
All inputs are finite; a program needn't handle non-finite values.
Results may differ from the reference program's by a relative error of at most 0.006.
Values may be sent and summed in bfloat16 or wider, within the bound.
A program may use at most 64 MiB of HBM per device.

```python
import math
import jax
import jax.numpy as jnp
from jax import lax

TRUNC = 256
NLON = 768
FIELDS = 4
HIDDEN_SIZE = 512
WAVE_DEV = 8
NLAT = 256
NLEV = 24
FEAT = 96
N_LAT = 32


def draw_wave_order(key, part):
    owners = jax.random.permutation(jax.random.fold_in(key, 11), N_LAT).astype(jnp.int32)
    groups = jnp.arange(WAVE_DEV, dtype=jnp.int32)
    position = jnp.where(groups[None, :] % 2 == 0, owners[:, None], N_LAT - 1 - owners[:, None])
    return (groups[None, :] * N_LAT + position).reshape(TRUNC).astype(jnp.int32)


def steps_of(own_key, extent, cuts, least, top_value):
    level, own = 1.0, jax.random.fold_in(own_key, 6)
    for dim, shards_of in cuts:
        heights = jnp.exp(jax.random.uniform(jax.random.fold_in(own, dim), (shards_of,), jnp.float32, least / len(cuts), top_value / len(cuts)))
        level = level * jnp.repeat(heights, extent[dim] // shards_of).reshape([-1 if axis == dim else 1 for axis in range(len(extent))])
    return level


def gaussian(key, shape, spread, most, pieces=(), kind=jnp.bfloat16):
    factor_of = steps_of(key, shape, pieces, -0.22, 0.18) if pieces else 1.0
    array = jax.random.normal(key, shape, jnp.float32) * spread * factor_of
    return jnp.minimum(jnp.maximum(array, -most), most).astype(kind)


def setup_inputs(seed: int = 0) -> dict:
    seeds = jax.random.split(jax.random.key(seed), 12)
    return {
        "prognostic": gaussian(seeds[0], (FIELDS, NLEV, NLAT, NLON), 1.0, 6.0, ((1, 8), (2, 32)), jnp.float32),
        "cotangent": gaussian(seeds[1], (FIELDS, NLEV, NLAT, NLON), 1.0, 6.0, ((1, 8), (2, 32))),
        "damping": jnp.clip(jnp.exp(math.log(30.0) - 3.4011974 * jax.random.uniform(seeds[2], (FIELDS, NLEV), jnp.float32) ** steps_of(seeds[2], (FIELDS, NLEV), ((1, 8),), -0.2, 0.2)), 1.0, 30.0),
        "in_scale": jnp.clip(jnp.exp(jax.random.uniform(seeds[3], (FIELDS, NLEV), jnp.float32, math.log(0.5), math.log(4.0))), 0.5, 4.0),
        "w_in": gaussian(seeds[4], (HIDDEN_SIZE, FEAT), FEAT ** -0.5, 0.625),
        "b_in": gaussian(seeds[5], (HIDDEN_SIZE,), 0.5, 3.0, (), jnp.float32),
        "w_mid": gaussian(seeds[6], (HIDDEN_SIZE, HIDDEN_SIZE), HIDDEN_SIZE ** -0.5, 0.25),
        "b_mid": gaussian(seeds[7], (HIDDEN_SIZE,), 0.5, 3.0, (), jnp.float32),
        "w_out": gaussian(seeds[8], (FEAT, HIDDEN_SIZE), HIDDEN_SIZE ** -0.5, 0.25),
        "wave_order": draw_wave_order(jax.random.fold_in(seeds[11], 71), 0),
        "lat_order": jax.random.permutation(seeds[10], NLAT).astype(jnp.int32),
    }


block_rows = 32
rescale_bits = 40.0

def legendre_setup(own_waves, colatitude):
    float_type = colatitude.dtype
    all_orders = jnp.arange(TRUNC, dtype=jnp.int32)
    factor_index = jnp.arange(1, TRUNC, dtype=jnp.int32).astype(float_type)
    ratios = 0.5 * jnp.log((2.0 * factor_index + 1.0) / (2.0 * factor_index))
    totals = jnp.concatenate([jnp.zeros((1,), float_type), jnp.cumsum(ratios)])
    matches = own_waves[:, None] == all_orders[None, :]
    diagonal_log = lax.optimization_barrier(jnp.sum(jnp.where(matches, totals[None, :], 0.0), axis=1)) - 0.5 * math.log(2.0)
    orders = own_waves.astype(float_type)
    log_shift = diagonal_log[:, None] + orders[:, None] * jnp.log(jnp.sin(colatitude))[None, :]
    empty_rows = jnp.zeros_like(log_shift)
    return (empty_rows, empty_rows, log_shift)

def legendre_rows(recurrence, first_degree, orders, cosine):
    latest, before, log_shift = recurrence
    rescale_limit = 2.0 ** rescale_bits
    squared_order = orders * orders
    table_rows = []
    for offset in range(block_rows):
        degree = (first_degree + offset).astype(cosine.dtype)
        upper_coef = jnp.sqrt(jnp.maximum(4.0 * degree * degree - 1.0, 0.0) / jnp.maximum(degree * degree - squared_order, 1.0))
        lower_num = jnp.maximum((degree - 1.0) * (degree - 1.0) - squared_order, 0.0)
        lower_coef = jnp.sqrt(lower_num / jnp.maximum(4.0 * (degree - 1.0) * (degree - 1.0) - 1.0, 1.0))
        recurred = upper_coef[:, None] * (cosine[None, :] * latest - lower_coef[:, None] * before)
        diagonal_start = jnp.where(degree == orders, 1.0, 0.0)[:, None] * jnp.ones_like(latest)
        newest = jnp.where((degree > orders)[:, None], recurred, diagonal_start)
        too_large = jnp.abs(newest) > rescale_limit
        factor = jnp.where(too_large, 1.0 / rescale_limit, 1.0)
        newest = newest * factor
        latest = latest * factor
        log_shift = log_shift + jnp.where(too_large, rescale_bits * math.log(2.0), 0.0)
        table_rows.append(newest * jnp.exp(log_shift))
        before = latest
        latest = newest
    return ((latest, before, log_shift), jnp.stack(table_rows, axis=1))

def spectral_pass(own_waves, colatitude, fourier, damping):
    float_type = fourier.dtype
    lat_total = colatitude.shape[0]
    weight = math.pi / lat_total * jnp.sin(colatitude)
    cosine = jnp.cos(colatitude)
    orders = own_waves.astype(float_type)
    weighted = fourier * weight
    degree_norm = 1.0 / (TRUNC * (TRUNC - 1.0))

    def visit_block(carried, first_degree):
        recurrence, grid_sum = carried
        recurrence, legendre_table = legendre_rows(recurrence, first_degree, orders, cosine)
        coeffs = jnp.einsum('jbn,jkfen->jkfeb', legendre_table, weighted, precision=lax.Precision.HIGHEST)
        degree = (first_degree + jnp.arange(block_rows, dtype=jnp.int32)).astype(float_type)
        degree_ratio = degree * (degree + 1.0) * degree_norm
        coeffs = coeffs / (1.0 + damping[:, :, None] * (degree_ratio * degree_ratio)[None, None, :])
        grid_sum = grid_sum + jnp.einsum('jbn,jkfeb->jkfen', legendre_table, coeffs, precision=lax.Precision.HIGHEST)
        return ((recurrence, grid_sum), coeffs)
    starts = jnp.arange(0, TRUNC, block_rows, dtype=jnp.int32)
    initial = (legendre_setup(own_waves, colatitude), jnp.zeros_like(fourier))
    (recurrence, synthesized), blocks = lax.scan(visit_block, initial, starts)
    waves, two, fields, levels = fourier.shape[:4]
    coeffs = jnp.moveaxis(blocks, 0, 4).reshape(waves, two, fields, levels, TRUNC)
    return (coeffs, synthesized)

def silu_slope(value):
    sigmoid_value = jax.nn.sigmoid(value)
    return sigmoid_value * (1.0 + value * (1.0 - sigmoid_value))

def column_physics(inputs, upstream, w_in, b_in, w_mid, b_mid, w_out):
    pre_in = jnp.dot(w_in, inputs, preferred_element_type=jnp.float32) + b_in[:, None]
    hidden_in = jax.nn.silu(pre_in).astype(jnp.bfloat16)
    pre_mid = jnp.dot(w_mid, hidden_in, preferred_element_type=jnp.float32) + b_mid[:, None]
    hidden_mid = jax.nn.silu(pre_mid).astype(jnp.bfloat16)
    tendency = jnp.dot(w_out, hidden_mid, preferred_element_type=jnp.float32).astype(jnp.bfloat16)
    grad_out = jnp.dot(upstream, hidden_mid.T, preferred_element_type=jnp.float32)
    back_mid = jnp.dot(w_out.T, upstream, preferred_element_type=jnp.float32)
    delta_mid = (back_mid * silu_slope(pre_mid)).astype(jnp.bfloat16)
    grad_mid = jnp.dot(delta_mid, hidden_in.T, preferred_element_type=jnp.float32)
    grad_bmid = lax.optimization_barrier(jnp.sum(delta_mid.astype(jnp.float32), axis=1))
    back_in = jnp.dot(w_mid.T, delta_mid, preferred_element_type=jnp.float32)
    delta_in = (back_in * silu_slope(pre_in)).astype(jnp.bfloat16)
    grad_in = jnp.dot(delta_in, inputs.T, preferred_element_type=jnp.float32)
    grad_bin = lax.optimization_barrier(jnp.sum(delta_in.astype(jnp.float32), axis=1))
    return (tendency, (grad_in, grad_bin, grad_mid, grad_bmid, grad_out))

def physics_rows(inputs, upstream, w_in, b_in, w_mid, b_mid, w_out):
    fields, lev_total, lat_rows, lon_count = inputs.shape
    features = fields * lev_total
    hidden_units = w_in.shape[0]
    rows_in = jnp.moveaxis(inputs.reshape(features, lat_rows, lon_count), 1, 0)
    rows_up = jnp.moveaxis(upstream.reshape(features, lat_rows, lon_count), 1, 0)

    def visit_row(totals, row_pair):
        tendency, gradients = column_physics(row_pair[0], row_pair[1], w_in, b_in, w_mid, b_mid, w_out)
        return (jax.tree.map(jnp.add, totals, gradients), tendency)
    empty_sums = (jnp.zeros((hidden_units, features), jnp.float32), jnp.zeros((hidden_units,), jnp.float32), jnp.zeros((hidden_units, hidden_units), jnp.float32), jnp.zeros((hidden_units,), jnp.float32), jnp.zeros((features, hidden_units), jnp.float32))
    totals, tend_rows = lax.scan(visit_row, empty_sums, (rows_in, rows_up))
    tendency = jnp.moveaxis(tend_rows, 0, 1).reshape(fields, lev_total, lat_rows, lon_count)
    return (tendency, totals)

def reference(prognostic, cotangent, damping, in_scale, w_in, b_in, w_mid, b_mid, w_out, wave_order, lat_order):
    float_type = prognostic.dtype
    fields, lev_total, lat_total, lon_count = prognostic.shape
    colatitude = math.pi * (lat_order.astype(float_type) + 0.5) / lat_total
    spectrum = jnp.fft.rfft(prognostic, axis=3)[:, :, :, :TRUNC] / lon_count
    complex_parts = jnp.stack([jnp.real(spectrum), jnp.imag(spectrum)], axis=0).astype(float_type)
    fourier = jnp.transpose(complex_parts, (4, 0, 1, 2, 3))
    coeffs, synthesized = spectral_pass(jnp.arange(TRUNC, dtype=jnp.int32), colatitude, fourier, damping)
    spectral = jnp.take(coeffs, wave_order, axis=0)
    wave_modes = jnp.transpose(synthesized[:, 0] + 1j * synthesized[:, 1], (1, 2, 3, 0))
    padded = jnp.pad(wave_modes, ((0, 0), (0, 0), (0, 0), (0, lon_count // 2 + 1 - TRUNC)))
    filtered = (jnp.fft.irfft(padded, n=lon_count, axis=3) * lon_count).astype(float_type)
    inputs = (filtered * in_scale[:, :, None, None]).astype(jnp.bfloat16)
    tendency, totals = physics_rows(inputs, cotangent, w_in, b_in, w_mid, b_mid, w_out)
    new_state = filtered + tendency.astype(float_type)
    grad_scale = 1.0 / math.sqrt(lat_total * lon_count)
    gradients = jax.tree.map(lambda value: value * grad_scale, totals)
    return (new_state, spectral, gradients[0], gradients[1], gradients[2], gradients[3], gradients[4])
```

```python
import math

import jax
import jax.numpy as jnp
import numpy as np
from jax import lax
from jax.experimental import pallas as pl
from jax.experimental.pallas import tpu as pltpu
from jax.sharding import PartitionSpec as P

f32 = jnp.float32
bf16 = jnp.bfloat16

TRUNC = 256
NLON = 768
N_LAT = 32
N_LEV = 8
WAVES = 8
ROWS = 8
PAD = 16
USED = 12
HALF = TRUNC * WAVES
SCALE_BITS = 110
MESH = pl.DeviceIdType.MESH
VMEM = pl.BlockSpec(memory_space=pltpu.VMEM)
SMEM = pl.BlockSpec(memory_space=pltpu.SMEM)


def dft_tables():
    n = np.arange(NLON)[:, None]
    m = np.arange(TRUNC)[None, :]
    angle = 2.0 * np.pi * ((n * m) % NLON) / NLON
    table = np.concatenate([np.cos(angle), -np.sin(angle)], axis=1)
    high = table.astype(jnp.bfloat16)
    low = (table - high.astype(np.float64)).astype(jnp.bfloat16)
    return jnp.asarray(high), jnp.asarray(low)


def diagonal_table():
    index = np.arange(1, TRUNC, dtype=np.float64)
    ratios = 0.5 * np.log((2.0 * index + 1.0) / (2.0 * index))
    totals = np.concatenate([[0.0], np.cumsum(ratios)]) - 0.5 * np.log(2.0)
    return jnp.asarray(totals.astype(np.float32)[None, :])


def degree_table():
    degree = np.arange(TRUNC, dtype=np.float64)
    root = np.sqrt(np.maximum(4.0 * degree * degree - 1.0, 0.0))
    before = np.concatenate([[1.0], np.maximum(root[:-1], 1.0)])
    return jnp.asarray(np.stack([root, 1.0 / before]).astype(np.float32))


def iota(shape, axis):
    return lax.broadcasted_iota(jnp.int32, shape, axis)


def mm(a, b):
    return lax.dot_general(a, b, (((1,), (0,)), ((), ())), preferred_element_type=f32)


def mm_nt(a, b):
    return lax.dot_general(a, b, (((1,), (1,)), ((), ())), preferred_element_type=f32)


def split(value):
    high = value.astype(bf16)
    return high, (value - high.astype(f32)).astype(bf16)


def wave_onehot(order_ref):
    return (iota((TRUNC, TRUNC), 0) == order_ref[...]).astype(f32).astype(bf16)


def feature_of(column):
    lev, pair = column // PAD, column % PAD
    field = (
        (pair >= 3).astype(jnp.int32) + (pair >= 6).astype(jnp.int32) + (pair >= 9).astype(jnp.int32)
    )
    feature = field * 24 + lev * 3 + pair - field * 3
    return jnp.where(pair < USED, feature, -1)


def feature_onehot(shape, feature_axis):
    column = feature_of(iota(shape, 1 - feature_axis))
    return (iota(shape, feature_axis) == column).astype(f32).astype(bf16)


def take_rows(rows, source, target):
    for c in range(NLON // 128):
        rows[96 * c : 96 * (c + 1), :] = source[:, 128 * c : 128 * (c + 1)].astype(f32)
        for a in range(ROWS):
            picked = rows[pl.ds(96 * c + a, USED, stride=ROWS), :]
            target[PAD * a : PAD * a + USED, 128 * c : 128 * (c + 1)] = picked


def forward_kernel(
    x_ref, ct_ref, high_ref, low_ref, order_ref, lat_ref, four_ref, up_ref, rows, xs, fs
):
    lat = lax.axis_index("lat")
    xs[...] = jnp.zeros_like(xs)
    take_rows(rows, ct_ref, xs)
    for a in range(ROWS):
        up_ref[a] = xs[PAD * a : PAD * (a + 1), :].astype(bf16)
    take_rows(rows, x_ref, xs)
    xh, xl = split(xs[...])
    modes = mm(xh, high_ref[...]) + mm(xl, high_ref[...]) + mm(xh, low_ref[...])
    theta = (math.pi / 256.0) * (lat_ref[...].astype(f32) + 0.5)
    weight = (math.pi / 256.0 / NLON) * jnp.sin(theta)
    row = iota((ROWS * PAD, 256), 0) // PAD + lat * ROWS
    picked = jnp.where(iota((ROWS * PAD, 256), 1) == row, weight, 0.0)
    modes = (modes * jnp.sum(picked, axis=1, keepdims=True)).astype(bf16)
    onehot = wave_onehot(order_ref)
    for k in range(2):
        ordered = mm(modes[:, k * 256 : (k + 1) * 256], onehot)
        fs[:, 8 * k : 8 * (k + 1), :] = ordered.T.reshape(N_LAT, 8, 128)
    four_ref[...] = fs[...].astype(bf16)


def legendre_kernel(
    four_ref, order_ref, lat_ref, diag_ref, deg_ref, damp_ref, spec_ref, out_ref, table, rs, so
):
    lat = lax.axis_index("lat")
    lane = iota((WAVES, 256), 1)
    mine = lane == lat * WAVES + iota((WAVES, 256), 0)
    order = order_ref[...].astype(f32)
    wave = jnp.sum(jnp.where(mine, order, 0.0), axis=1, keepdims=True)
    diag_log = jnp.sum(
        jnp.where(lane.astype(f32) == wave, diag_ref[...], 0.0), axis=1, keepdims=True
    )
    source = (iota((256, 256), 1) % N_LAT) * ROWS + iota((256, 256), 1) // N_LAT
    reorder = (iota((256, 256), 0) == source).astype(f32).astype(bf16)
    lat_row = jnp.broadcast_to(lat_ref[...].astype(f32), (8, 256)).astype(bf16)
    theta = (math.pi / 256.0) * (mm(lat_row, reorder) + 0.5)
    cosine = jnp.cos(theta)
    start = jnp.exp(diag_log + wave * jnp.log(jnp.sin(theta)) + SCALE_BITS * math.log(2.0))
    wave128 = jnp.broadcast_to(wave, (WAVES, 128))
    square = wave128 * wave128
    descale = 2.0**-SCALE_BITS

    def step(degree, carried):
        latest, before, root_before = carried
        value = degree.astype(f32)
        gap = value * value - square
        safe = jnp.maximum(gap, 1.0)
        inverse = lax.rsqrt(safe)
        inverse = inverse * (1.5 - 0.5 * safe * inverse * inverse)
        root = jnp.maximum(gap, 0.0) * inverse
        upper = inverse * deg_ref[0, degree]
        lower = upper * root_before * deg_ref[1, degree]
        upper2 = jnp.concatenate([upper, upper], axis=1)
        lower2 = jnp.concatenate([lower, lower], axis=1)
        first = jnp.where(wave == value, start, 0.0)
        newest = (upper2 * cosine) * latest + (first - lower2 * before)
        scaled = newest * descale
        at = pl.multiple_of(degree * WAVES, WAVES)
        table[pl.ds(at, WAVES), :] = scaled[:, :128]
        table[pl.ds(at + HALF, WAVES), :] = scaled[:, 128:]
        return newest, latest, root

    table[0:WAVES, :] = jnp.zeros((WAVES, 128), f32)
    half = table[0:WAVES, :]
    zero = jnp.concatenate([half, half], axis=1)
    lax.fori_loop(0, TRUNC, step, (zero, zero, half), unroll=8)

    pair = iota((PAD, 256), 0)
    damping = jnp.zeros((PAD, 256), f32)
    for i in range(USED):
        damping = jnp.where(pair == i, damp_ref[i // 3, i % 3], damping)
    degree = iota((PAD, 256), 1).astype(f32)
    ratio = degree * (degree + 1.0) * (1.0 / (TRUNC * (TRUNC - 1.0)))
    response = 1.0 / (1.0 + damping * ratio * ratio)
    response = jnp.concatenate([response, response], axis=0)

    for i in range(N_LAT):
        rs[i] = four_ref[i].astype(f32)
    flat = rs.reshape(N_LAT * PAD, 128)
    turned = []
    for q in range(4):
        block = jnp.concatenate(
            [flat[pl.ds(4 * q + i, N_LAT, stride=PAD), :] for i in range(4)], axis=0
        )
        turned.append(block.T)

    def rows_of(kj):
        piece = turned[kj // 4]
        low = 32 * (kj % 4)
        return jnp.concatenate(
            [piece[PAD * a : PAD * (a + 1), low : low + 32] for a in range(ROWS)], axis=1
        )

    made = [None] * 16
    for j in range(WAVES):
        field = jnp.concatenate([rows_of(j), rows_of(8 + j)], axis=0).astype(bf16)
        left = table[pl.ds(j, TRUNC, stride=WAVES), :]
        right = table[pl.ds(HALF + j, TRUNC, stride=WAVES), :]
        high, low = split(jnp.concatenate([left, right], axis=1))
        coeffs = (mm_nt(field, high) + mm_nt(field, low)) * response
        for k in range(2):
            for f in range(4):
                at = PAD * k + 3 * f
                spec_ref[j, k, f] = coeffs[at : at + 3, :]
        ch, cl = split(coeffs)
        grid = mm(ch, high) + mm(cl, high) + mm(ch, low)
        made[j] = grid[:PAD]
        made[8 + j] = grid[PAD:]
    flat_out = so.reshape(N_LAT * PAD, 128)
    for q in range(4):
        block = jnp.concatenate(
            [
                jnp.concatenate(
                    [made[4 * q + i][:, 32 * a : 32 * (a + 1)] for i in range(4)], axis=1
                )
                for a in range(ROWS)
            ],
            axis=0,
        )
        back = block.T
        for i in range(4):
            flat_out[pl.ds(4 * q + i, N_LAT, stride=PAD), :] = back[32 * i : 32 * (i + 1)]
    out_ref[...] = so[...]


def inverse_kernel(syn_ref, high_ref, low_ref, order_ref, scale_ref, filt_ref, in_ref, turn):
    lev = lax.axis_index("lev")
    onehot = wave_onehot(order_ref)
    factor = jnp.where(iota((TRUNC, 128), 0) == 0, 1.0, 2.0)
    parts = []
    for k in range(2):
        part_high, part_low = split(syn_ref[:, 8 * k : 8 * (k + 1), :].reshape(TRUNC, 128))
        parts.append(((mm(onehot, part_high) + mm(onehot, part_low)) * factor).T)
    mh, ml = split(jnp.concatenate(parts, axis=1))
    rows = mm_nt(mh, high_ref[...]) + mm_nt(ml, high_ref[...]) + mm_nt(mh, low_ref[...])
    pair = iota((PAD, NLON), 0)
    scale = jnp.zeros((PAD, NLON), f32)
    for i in range(USED):
        scale = jnp.where(pair == i, scale_ref[i // 3, lev * 3 + i % 3], scale)
    for a in range(ROWS):
        piece = rows[PAD * a : PAD * (a + 1), :]
        for c in range(NLON // 128):
            turn[pl.ds(96 * c + a, USED, stride=ROWS), :] = piece[:USED, 128 * c : 128 * (c + 1)]
        in_ref[a] = (piece * scale).astype(bf16)
    for c in range(NLON // 128):
        filt_ref[:, 128 * c : 128 * (c + 1)] = turn[96 * c : 96 * (c + 1), :]


def network_kernel(
    in_ref, up_ref, win_ref, bin_ref, wmid_ref, bmid_ref, wout_ref, tend_ref, grad_ref,
    win_s, wout_s, woutT_s, wmidT_s, bin_s, bmid_s, in_s, up_s, tend_s, gin, gmid, gout, gbm,
):
    win_s[...] = mm(win_ref[...], feature_onehot((96, 128), 0)).astype(bf16)
    wout = mm(feature_onehot((128, 96), 1), wout_ref[...])
    wout_s[...] = wout.astype(bf16)
    woutT_s[...] = wout.T.astype(bf16)
    wmidT_s[...] = wmid_ref[...].astype(f32).T.astype(bf16)
    bin_s[...] = jnp.broadcast_to(bin_ref[...], (128, 512)).T
    bmid_s[...] = jnp.broadcast_to(bmid_ref[...], (128, 512)).T
    inputs = in_ref[...].reshape(128, NLON)
    in_s[...] = jnp.where(iota((128, NLON), 0) == USED, 1.0, inputs.astype(f32)).astype(bf16)
    up_s[...] = up_ref[...].reshape(128, NLON)
    gin[...] = jnp.zeros_like(gin)
    gmid[...] = jnp.zeros_like(gmid)
    gout[...] = jnp.zeros_like(gout)
    gbm[...] = jnp.zeros_like(gbm)

    def activation(value):
        z = 0.5 + 0.5 * jnp.tanh(0.5 * value)
        return value * z, z * (1.0 + value * (1.0 - z))

    def chunk(c, _):
        cols = pl.ds(pl.multiple_of(c * 256, 256), 256)
        inp, up = in_s[:, cols], up_s[:, cols]
        b_in = jnp.concatenate([bin_s[...], bin_s[...]], axis=1)
        h_in, slope_in = activation(mm(win_s[...], inp) + b_in)
        h_in = h_in.astype(bf16)
        b_mid = jnp.concatenate([bmid_s[...], bmid_s[...]], axis=1)
        h_mid, slope_mid = activation(mm(wmid_ref[...], h_in) + b_mid)
        h_mid = h_mid.astype(bf16)
        tend_s[:, cols] = mm(wout_s[...], h_mid).astype(bf16)
        gout[...] += mm_nt(h_mid, up)
        d_mid = (mm(woutT_s[...], up) * slope_mid).astype(bf16)
        gmid[...] += mm_nt(d_mid, h_in)
        wide = d_mid.astype(f32)
        gbm[...] += wide[:, :128] + wide[:, 128:]
        d_in = (mm(wmidT_s[...], d_mid) * slope_in).astype(bf16)
        gin[...] += mm_nt(d_in, inp)
        return 0

    lax.fori_loop(0, 3, chunk, 0)
    tend_ref[...] = tend_s[...].reshape(N_LEV, PAD, NLON)
    norm = 1.0 / math.sqrt(256 * NLON)
    bias = jnp.sum(gbm[...], axis=1, keepdims=True)
    last = jnp.where(iota((512, 128), 1) == USED, bias, gout[...])
    grad_ref[:, :, 0:128] = (gin[...] * norm).astype(bf16).reshape(N_LAT, 16, 128)
    grad_ref[:, :, 128:640] = (gmid[...] * norm).astype(bf16).reshape(N_LAT, 16, 512)
    grad_ref[:, :, 640:768] = (last * norm).astype(bf16).reshape(N_LAT, 16, 128)


def finish_kernel(
    filt_ref, tend_ref, grad_ref, state_ref, gin_ref, gbin_ref, gmid_ref, gbmid_ref, gout_ref, turn
):
    for a in range(ROWS):
        piece = tend_ref[a].astype(f32)
        for c in range(NLON // 128):
            turn[pl.ds(96 * c + a, USED, stride=ROWS), :] = piece[:USED, 128 * c : 128 * (c + 1)]
    for c in range(NLON // 128):
        cols = slice(128 * c, 128 * (c + 1))
        state_ref[:, cols] = filt_ref[:, cols] + turn[96 * c : 96 * (c + 1), :]
    total = grad_ref[...].reshape(512, NLON)
    first, last = total[:, :128], total[:, 640:]
    gin_ref[...] = mm(first, feature_onehot((128, 96), 1))
    gout_ref[...] = mm_nt(feature_onehot((96, 128), 0), last)
    gmid_ref[...] = total[:, 128:640].astype(f32)
    pick = (iota((8, 128), 1) == USED).astype(f32).astype(bf16)
    gbin_ref[...] = mm_nt(pick, first)[:1]
    gbmid_ref[...] = mm_nt(pick, last)[:1]


def greet(axes):
    barrier = pltpu.get_barrier_semaphore()
    for axis, size in axes:
        me = lax.axis_index(axis)

        def signal(d, _):
            peer = lax.rem(me + d, size)
            pl.semaphore_signal(barrier, inc=1, device_id={axis: peer}, device_id_type=MESH)
            return 0

        lax.fori_loop(1, size, signal, 0)
    pl.semaphore_wait(barrier, sum(size - 1 for _, size in axes))


def scatter(axis, size, source, landing, send, recv):
    me = lax.axis_index(axis)

    def copy(d):
        peer = lax.rem(me + d, size)
        return pltpu.make_async_remote_copy(
            src_ref=source(peer), dst_ref=landing.at[me], send_sem=send.at[d],
            recv_sem=recv.at[d], device_id={axis: peer}, device_id_type=MESH,
        )

    def start(d, _):
        copy(d).start()
        return 0

    def wait(d, _):
        copy(d).wait()
        return 0

    lax.fori_loop(1, size, start, 0)
    return lambda: lax.fori_loop(1, size, wait, 0)


def exchange_two_kernel(four, up, four_out, up_out, s0, r0, s1, r1):
    greet((("lat", N_LAT), ("lev", N_LEV)))
    wait_up = scatter("lev", N_LEV, lambda p: up.at[p], up_out, s1, r1)
    wait_four = scatter("lat", N_LAT, lambda p: four.at[p], four_out, s0, r0)
    lat, lev = lax.axis_index("lat"), lax.axis_index("lev")
    four_out[lat] = four[lat]
    up_out[lev] = up[lev]
    wait_four()
    wait_up()


def exchange_kernel(axis, size, block, block_out, send, recv):
    greet(((axis, size),))
    wait = scatter(axis, size, lambda p: block.at[p], block_out, send, recv)
    me = lax.axis_index(axis)
    block_out[me] = block[me]
    wait()


def reduce_kernel(tend, grad, tend_out, total, parts, piece, pieces, done, s0, r0, s1, r1, s2, r2, s3, r3):
    greet((("lat", N_LAT), ("lev", N_LEV)))
    lat, lev = lax.axis_index("lat"), lax.axis_index("lev")
    wait_tend = scatter("lev", N_LEV, lambda p: tend.at[p], tend_out, s0, r0)
    wait_parts = scatter("lat", N_LAT, lambda p: grad.at[p], parts, s1, r1)
    tend_out[lev] = tend[lev]
    parts[lat] = grad[lat]
    wait_parts()

    def add(ref):
        def body(i, acc):
            return acc + ref[i].astype(f32)

        return body

    piece[...] = lax.fori_loop(1, N_LAT, add(parts), parts[0].astype(f32)).astype(bf16)
    wait_pieces = scatter("lev", N_LEV, lambda p: piece, pieces, s2, r2)
    pieces[lev] = piece[...]
    wait_pieces()
    done[...] = lax.fori_loop(1, N_LEV, add(pieces), pieces[0].astype(f32)).astype(bf16)
    wait_total = scatter("lat", N_LAT, lambda p: done, total, s3, r3)
    total[lat] = done[...]
    wait_total()
    wait_tend()


def like(shape, dtype):
    return jax.ShapeDtypeStruct(shape, dtype)


def local(kernel, out_shape, scratch, in_specs, name):
    return pl.pallas_call(
        kernel,
        out_shape=out_shape,
        in_specs=in_specs,
        out_specs=jax.tree.map(lambda _: VMEM, out_shape),
        scratch_shapes=scratch,
        name=name,
    )


def remote(kernel, out_shape, scratch, count, number, name):
    return pl.pallas_call(
        kernel,
        out_shape=out_shape,
        in_specs=[VMEM] * count,
        out_specs=jax.tree.map(lambda _: VMEM, out_shape),
        scratch_shapes=scratch,
        compiler_params=pltpu.CompilerParams(collective_id=number, has_side_effects=True),
        name=name,
    )


def sems(count):
    return [pltpu.SemaphoreType.DMA((count,)), pltpu.SemaphoreType.DMA((count,))]


def on_device(
    prognostic, cotangent, damping, in_scale, w_in, b_in, w_mid, b_mid, w_out, wave_order, lat_order
):
    high, low = dft_tables()
    order = wave_order.reshape(1, TRUNC)
    lats = lat_order.reshape(1, 256)
    rows96 = ROWS * USED
    waves_block = like((N_LAT, PAD, 128), bf16)
    wide_block = like((N_LAT, PAD, 128), f32)
    rows_block = like((N_LEV, PAD, NLON), bf16)

    four, up = local(
        forward_kernel, (waves_block, rows_block),
        [pltpu.VMEM((576, 128), f32), pltpu.VMEM((128, NLON), f32), pltpu.VMEM((N_LAT, PAD, 128), f32)],
        [VMEM] * 6, "forward",
    )(prognostic.reshape(rows96, NLON), cotangent.reshape(rows96, NLON), high, low, order, lats)

    four, up = remote(
        exchange_two_kernel, (waves_block, rows_block), sems(N_LAT) + sems(N_LEV), 2, 0, "exchange_a"
    )(four, up)

    spectral, synth = local(
        legendre_kernel, (like((WAVES, 2, 4, 3, TRUNC), f32), wide_block),
        [pltpu.VMEM((2 * HALF, 128), f32), pltpu.VMEM((N_LAT, PAD, 128), f32),
         pltpu.VMEM((N_LAT, PAD, 128), f32)],
        [VMEM] * 4 + [SMEM] * 2, "legendre",
    )(four, order, lats, diagonal_table(), degree_table(), damping)

    synth = remote(
        lambda *refs: exchange_kernel("lat", N_LAT, *refs), wide_block, sems(N_LAT), 1, 1, "exchange_b"
    )(synth)

    filtered, inputs = local(
        inverse_kernel, (like((rows96, NLON), f32), rows_block),
        [pltpu.VMEM((576, 128), f32)], [VMEM] * 4 + [SMEM], "inverse",
    )(synth, high, low, order, in_scale)

    inputs = remote(
        lambda *refs: exchange_kernel("lev", N_LEV, *refs), rows_block, sems(N_LEV), 1, 2, "exchange_c"
    )(inputs)

    grad_block = like((N_LAT, 16, NLON), bf16)
    tendency, grads = local(
        network_kernel, (rows_block, grad_block),
        [pltpu.VMEM((512, 128), bf16), pltpu.VMEM((128, 512), bf16), pltpu.VMEM((512, 128), bf16),
         pltpu.VMEM((512, 512), bf16), pltpu.VMEM((512, 128), f32), pltpu.VMEM((512, 128), f32),
         pltpu.VMEM((128, NLON), bf16), pltpu.VMEM((128, NLON), bf16), pltpu.VMEM((128, NLON), bf16),
         pltpu.VMEM((512, 128), f32), pltpu.VMEM((512, 512), f32), pltpu.VMEM((512, 128), f32),
         pltpu.VMEM((512, 128), f32)],
        [VMEM] * 7, "network",
    )(inputs, up, w_in, b_in.reshape(1, 512), w_mid, b_mid.reshape(1, 512), w_out)

    tendency, grads = remote(
        reduce_kernel, (rows_block, grad_block),
        [pltpu.VMEM((N_LAT, 16, NLON), bf16), pltpu.VMEM((16, NLON), bf16),
         pltpu.VMEM((N_LEV, 16, NLON), bf16), pltpu.VMEM((16, NLON), bf16)]
        + sems(N_LEV) + sems(N_LAT) + sems(N_LEV) + sems(N_LAT),
        2, 3, "exchange_d",
    )(tendency, grads)

    state, gin, gbin, gmid, gbmid, gout = local(
        finish_kernel,
        (like((rows96, NLON), f32), like((512, 96), f32), like((1, 512), f32),
         like((512, 512), f32), like((1, 512), f32), like((96, 512), f32)),
        [pltpu.VMEM((576, 128), f32)], [VMEM] * 3, "finish",
    )(filtered, tendency, grads)
    return (
        state.reshape(prognostic.shape), spectral, gin, gbin.reshape(512), gmid, gbmid.reshape(512), gout,
    )


def solution(mesh):
    return jax.shard_map(
        on_device,
        mesh=mesh,
        in_specs=(
            P(None, "lev", "lat", None),
            P(None, "lev", "lat", None),
            P(None, "lev"),
            P(),
            P(),
            P(),
            P(),
            P(),
            P(),
            P(),
            P(),
        ),
        out_specs=(
            P(None, "lev", "lat", None),
            P("lat", None, None, "lev", None),
            P(),
            P(),
            P(),
            P(),
            P(),
        ),
        check_vma=False,
    )
```

```python
import math

import jax
import jax.numpy as jnp
import numpy as np
from jax import lax
from jax.experimental import pallas as pl
from jax.experimental.pallas import tpu as pltpu
from jax.sharding import PartitionSpec as P

f32 = jnp.float32
bf16 = jnp.bfloat16

TRUNC = 256
NLON = 768
N_LAT = 32
N_LEV = 8
WAVES = 8
ROWS = 8
PAD = 16
USED = 12
HALF = TRUNC * WAVES
SCALE_BITS = 110
MESH = pl.DeviceIdType.MESH
VMEM = pl.BlockSpec(memory_space=pltpu.VMEM)
SMEM = pl.BlockSpec(memory_space=pltpu.SMEM)


def dft_tables():
    n = np.arange(NLON)[:, None]
    m = np.arange(TRUNC)[None, :]
    angle = 2.0 * np.pi * ((n * m) % NLON) / NLON
    table = np.concatenate([np.cos(angle), -np.sin(angle)], axis=1)
    high = table.astype(jnp.bfloat16)
    low = (table - high.astype(np.float64)).astype(jnp.bfloat16)
    return jnp.asarray(high), jnp.asarray(low)


def diagonal_table():
    index = np.arange(1, TRUNC, dtype=np.float64)
    ratios = 0.5 * np.log((2.0 * index + 1.0) / (2.0 * index))
    totals = np.concatenate([[0.0], np.cumsum(ratios)]) - 0.5 * np.log(2.0)
    return jnp.asarray(totals.astype(np.float32)[None, :])


def degree_table():
    degree = np.arange(TRUNC, dtype=np.float64)
    root = np.sqrt(np.maximum(4.0 * degree * degree - 1.0, 0.0))
    before = np.concatenate([[1.0], np.maximum(root[:-1], 1.0)])
    return jnp.asarray(np.stack([root, 1.0 / before]).astype(np.float32))


def iota(shape, axis):
    return lax.broadcasted_iota(jnp.int32, shape, axis)


def mm(a, b):
    return lax.dot_general(a, b, (((1,), (0,)), ((), ())), preferred_element_type=f32)


def mm_nt(a, b):
    return lax.dot_general(a, b, (((1,), (1,)), ((), ())), preferred_element_type=f32)


def split(value):
    high = value.astype(bf16)
    return high, (value - high.astype(f32)).astype(bf16)


def wave_onehot(order_ref):
    return (iota((TRUNC, TRUNC), 0) == order_ref[...]).astype(f32).astype(bf16)


def feature_of(column):
    lev, pair = column // PAD, column % PAD
    field = (
        (pair >= 3).astype(jnp.int32) + (pair >= 6).astype(jnp.int32) + (pair >= 9).astype(jnp.int32)
    )
    feature = field * 24 + lev * 3 + pair - field * 3
    return jnp.where(pair < USED, feature, -1)


def feature_onehot(shape, feature_axis):
    column = feature_of(iota(shape, 1 - feature_axis))
    return (iota(shape, feature_axis) == column).astype(f32).astype(bf16)


def take_rows(rows, source, target):
    for c in range(NLON // 128):
        rows[96 * c : 96 * (c + 1), :] = source[:, 128 * c : 128 * (c + 1)].astype(f32)
        for a in range(ROWS):
            picked = rows[pl.ds(96 * c + a, USED, stride=ROWS), :]
            target[PAD * a : PAD * a + USED, 128 * c : 128 * (c + 1)] = picked


def forward(x_ref, high_ref, low_ref, order_ref, lat_ref, rows, xs, fs, four_ref, lat):
    take_rows(rows, x_ref, xs)
    xh, xl = split(xs[...])
    modes = mm(xh, high_ref[...]) + mm(xl, high_ref[...]) + mm(xh, low_ref[...])
    theta = (math.pi / 256.0) * (lat_ref[...].astype(f32) + 0.5)
    weight = (math.pi / 256.0 / NLON) * jnp.sin(theta)
    row = iota((ROWS * PAD, 256), 0) // PAD + lat * ROWS
    picked = jnp.where(iota((ROWS * PAD, 256), 1) == row, weight, 0.0)
    modes = (modes * jnp.sum(picked, axis=1, keepdims=True)).astype(bf16)
    onehot = wave_onehot(order_ref)
    for k in range(2):
        ordered = mm(modes[:, k * 256 : (k + 1) * 256], onehot)
        fs[:, 8 * k : 8 * (k + 1), :] = ordered.T.reshape(N_LAT, 8, 128)
    four_ref[...] = fs[...].astype(bf16)


def legendre_table(order_ref, lat_ref, diag_ref, deg_ref, table, lat):
    lane = iota((WAVES, 256), 1)
    mine = lane == lat * WAVES + iota((WAVES, 256), 0)
    order = order_ref[...].astype(f32)
    wave = jnp.sum(jnp.where(mine, order, 0.0), axis=1, keepdims=True)
    diag_log = jnp.sum(
        jnp.where(lane.astype(f32) == wave, diag_ref[...], 0.0), axis=1, keepdims=True
    )
    source = (iota((256, 256), 1) % N_LAT) * ROWS + iota((256, 256), 1) // N_LAT
    reorder = (iota((256, 256), 0) == source).astype(f32).astype(bf16)
    lat_row = jnp.broadcast_to(lat_ref[...].astype(f32), (8, 256)).astype(bf16)
    theta = (math.pi / 256.0) * (mm(lat_row, reorder) + 0.5)
    cosine = jnp.cos(theta)
    start = jnp.exp(diag_log + wave * jnp.log(jnp.sin(theta)) + SCALE_BITS * math.log(2.0))
    wave128 = jnp.broadcast_to(wave, (WAVES, 128))
    square = wave128 * wave128
    descale = 2.0**-SCALE_BITS

    def step(degree, carried):
        latest, before, root_before = carried
        value = degree.astype(f32)
        gap = value * value - square
        safe = jnp.maximum(gap, 1.0)
        inverse = lax.rsqrt(safe)
        inverse = inverse * (1.5 - 0.5 * safe * inverse * inverse)
        root = jnp.maximum(gap, 0.0) * inverse
        upper = inverse * deg_ref[0, degree]
        lower = upper * root_before * deg_ref[1, degree]
        upper2 = jnp.concatenate([upper, upper], axis=1)
        lower2 = jnp.concatenate([lower, lower], axis=1)
        first = jnp.where(wave == value, start, 0.0)
        newest = (upper2 * cosine) * latest + (first - lower2 * before)
        scaled = newest * descale
        at = pl.multiple_of(degree * WAVES, WAVES)
        table[pl.ds(at, WAVES), :] = scaled[:, :128]
        table[pl.ds(at + HALF, WAVES), :] = scaled[:, 128:]
        return newest, latest, root

    table[0:WAVES, :] = jnp.zeros((WAVES, 128), f32)
    half = table[0:WAVES, :]
    zero = jnp.concatenate([half, half], axis=1)
    lax.fori_loop(0, TRUNC, step, (zero, zero, half), unroll=8)


def analysis(four_ref, damp_ref, spec_ref, table, rs, so):
    pair = iota((PAD, 256), 0)
    damping = jnp.zeros((PAD, 256), f32)
    for i in range(USED):
        damping = jnp.where(pair == i, damp_ref[i // 3, i % 3], damping)
    degree = iota((PAD, 256), 1).astype(f32)
    ratio = degree * (degree + 1.0) * (1.0 / (TRUNC * (TRUNC - 1.0)))
    response = 1.0 / (1.0 + damping * ratio * ratio)
    response = jnp.concatenate([response, response], axis=0)

    for i in range(N_LAT):
        rs[i] = four_ref[i].astype(f32)
    flat = rs.reshape(N_LAT * PAD, 128)
    turned = []
    for q in range(4):
        block = jnp.concatenate(
            [flat[pl.ds(4 * q + i, N_LAT, stride=PAD), :] for i in range(4)], axis=0
        )
        turned.append(block.T)

    def rows_of(kj):
        piece = turned[kj // 4]
        low = 32 * (kj % 4)
        return jnp.concatenate(
            [piece[PAD * a : PAD * (a + 1), low : low + 32] for a in range(ROWS)], axis=1
        )

    made = [None] * 16
    for j in range(WAVES):
        field = jnp.concatenate([rows_of(j), rows_of(8 + j)], axis=0).astype(bf16)
        left = table[pl.ds(j, TRUNC, stride=WAVES), :]
        right = table[pl.ds(HALF + j, TRUNC, stride=WAVES), :]
        high, low = split(jnp.concatenate([left, right], axis=1))
        coeffs = (mm_nt(field, high) + mm_nt(field, low)) * response
        for k in range(2):
            for f in range(4):
                at = PAD * k + 3 * f
                spec_ref[j, k, f] = coeffs[at : at + 3, :]
        ch, cl = split(coeffs)
        grid = mm(ch, high) + mm(cl, high) + mm(ch, low)
        made[j] = grid[:PAD]
        made[8 + j] = grid[PAD:]
    flat_out = so.reshape(N_LAT * PAD, 128)
    for q in range(4):
        block = jnp.concatenate(
            [
                jnp.concatenate(
                    [made[4 * q + i][:, 32 * a : 32 * (a + 1)] for i in range(4)], axis=1
                )
                for a in range(ROWS)
            ],
            axis=0,
        )
        back = block.T
        for i in range(4):
            flat_out[pl.ds(4 * q + i, N_LAT, stride=PAD), :] = back[32 * i : 32 * (i + 1)]


def inverse(syn_ref, high_ref, low_ref, order_ref, scale_ref, in_ref, turn, lev):
    onehot = wave_onehot(order_ref)
    factor = jnp.where(iota((TRUNC, 128), 0) == 0, 1.0, 2.0)
    parts = []
    for k in range(2):
        part_high, part_low = split(syn_ref[:, 8 * k : 8 * (k + 1), :].reshape(TRUNC, 128))
        parts.append(((mm(onehot, part_high) + mm(onehot, part_low)) * factor).T)
    mh, ml = split(jnp.concatenate(parts, axis=1))
    rows = mm_nt(mh, high_ref[...]) + mm_nt(ml, high_ref[...]) + mm_nt(mh, low_ref[...])
    pair = iota((PAD, NLON), 0)
    scale = jnp.zeros((PAD, NLON), f32)
    for i in range(USED):
        scale = jnp.where(pair == i, scale_ref[i // 3, lev * 3 + i % 3], scale)
    for a in range(ROWS):
        piece = rows[PAD * a : PAD * (a + 1), :]
        in_ref[a] = (piece * scale).astype(bf16)
        for c in range(NLON // 128):
            turn[pl.ds(96 * c + a, USED, stride=ROWS), :] = piece[:USED, 128 * c : 128 * (c + 1)]


def prepare(win_ref, bin_ref, wmid_ref, bmid_ref, wout_ref, win_s, wout_s, woutT_s, wmidT_s, bin_s, bmid_s):
    win_s[...] = mm(win_ref[...], feature_onehot((96, 128), 0)).astype(bf16)
    wout = mm(feature_onehot((128, 96), 1), wout_ref[...])
    wout_s[...] = wout.astype(bf16)
    woutT_s[...] = wout.T.astype(bf16)
    wmidT_s[...] = wmid_ref[...].astype(f32).T.astype(bf16)
    bin_s[...] = jnp.broadcast_to(bin_ref[...], (128, 512)).T
    bmid_s[...] = jnp.broadcast_to(bmid_ref[...], (128, 512)).T


def activation(value):
    z = 0.5 + 0.5 * jnp.tanh(0.5 * value)
    return value * z, z * (1.0 + value * (1.0 - z))


def columns(c):
    return pl.ds(pl.multiple_of(c * 256, 256), 256)


def greet(axes):
    barrier = pltpu.get_barrier_semaphore()
    for axis, size in axes:
        me = lax.axis_index(axis)

        def signal(d, _):
            peer = lax.rem(me + d, size)
            pl.semaphore_signal(barrier, inc=1, device_id={axis: peer}, device_id_type=MESH)
            return 0

        lax.fori_loop(1, size, signal, 0)
    return lambda: pl.semaphore_wait(barrier, sum(size - 1 for _, size in axes))


def scatter(axis, size, source, landing, send, recv):
    me = lax.axis_index(axis)

    def copy(d):
        peer = lax.rem(me + d, size)
        return pltpu.make_async_remote_copy(
            src_ref=source(peer), dst_ref=landing.at[me], send_sem=send.at[d],
            recv_sem=recv.at[d], device_id={axis: peer}, device_id_type=MESH,
        )

    def start(d, _):
        copy(d).start()
        return 0

    def wait(d, _):
        copy(d).wait()
        return 0

    lax.fori_loop(1, size, start, 0)
    return lambda: lax.fori_loop(1, size, wait, 0)


def total_of(ref):
    def body(i, acc):
        return acc + ref[i].astype(f32)

    return lax.fori_loop(1, ref.shape[0], body, ref[0].astype(f32))


def step_kernel(
    x_ref, ct_ref, high_ref, low_ref, order_ref, lat_ref, diag_ref, deg_ref, damp_ref, scale_ref,
    win_ref, bin_ref, wmid_ref, bmid_ref, wout_ref,
    spec_ref, state_ref, tot0, tot1, tot2, tot3,
    rows, xs, fs, up_send, up_in, four_send, four_in, table, so, syn_in, turn, in_send, in_in,
    win_s, wout_s, woutT_s, wmidT_s, bin_s, bmid_s, in_s, up_s, bm_s, h_in_s, slope_s, h_mid_s,
    d_mid_s, d_in_s, gbm, tend_s, tend_send, tend_in,
    send0, send1, send2, send3, part0, part1, part2, part3,
    piece0, piece1, piece2, piece3, pieces0, pieces1, pieces2, pieces3, done0, done1, done2, done3,
    *semaphores,
):
    lat, lev = lax.axis_index("lat"), lax.axis_index("lev")
    pairs = iter([semaphores[i : i + 2] for i in range(0, len(semaphores), 2)])
    met = greet((("lat", N_LAT), ("lev", N_LEV)))

    def to_lat(source, landing):
        return scatter("lat", N_LAT, source, landing, *next(pairs))

    def to_lev(source, landing):
        return scatter("lev", N_LEV, source, landing, *next(pairs))

    xs[...] = jnp.zeros_like(xs)
    take_rows(rows, ct_ref, xs)
    for a in range(ROWS):
        up_send[a] = xs[PAD * a : PAD * (a + 1), :].astype(bf16)
    forward(x_ref, high_ref, low_ref, order_ref, lat_ref, rows, xs, fs, four_send, lat)
    met()
    wait_four = to_lat(lambda p: four_send.at[p], four_in)
    wait_up = to_lev(lambda p: up_send.at[p], up_in)
    four_in[lat] = four_send[lat]
    up_in[lev] = up_send[lev]
    legendre_table(order_ref, lat_ref, diag_ref, deg_ref, table, lat)
    wait_four()
    analysis(four_in, damp_ref, spec_ref, table, fs, so)
    wait_syn = to_lat(lambda p: so.at[p], syn_in)
    syn_in[lat] = so[lat]
    prepare(
        win_ref, bin_ref, wmid_ref, bmid_ref, wout_ref, win_s, wout_s, woutT_s, wmidT_s, bin_s, bmid_s
    )
    wait_syn()
    inverse(syn_in, high_ref, low_ref, order_ref, scale_ref, in_send, turn, lev)
    wait_in = to_lev(lambda p: in_send.at[p], in_in)
    in_in[lev] = in_send[lev]
    wait_up()
    up_s[...] = up_in[...].reshape(128, NLON)

    def back_chunk(c, _):
        bm_s[:, columns(c)] = mm(woutT_s[...], up_s[:, columns(c)])
        return 0

    lax.fori_loop(0, 3, back_chunk, 0)
    gbm[...] = jnp.zeros_like(gbm)
    wait_in()
    inputs = in_in[...].reshape(128, NLON)
    in_s[...] = jnp.where(iota((128, NLON), 0) == USED, 1.0, inputs.astype(f32)).astype(bf16)

    def chunk(c, _):
        cols = columns(c)
        b_in = jnp.concatenate([bin_s[...], bin_s[...]], axis=1)
        h_in, slope_in = activation(mm(win_s[...], in_s[:, cols]) + b_in)
        h_in = h_in.astype(bf16)
        h_in_s[:, cols] = h_in
        slope_s[:, cols] = slope_in
        b_mid = jnp.concatenate([bmid_s[...], bmid_s[...]], axis=1)
        h_mid, slope_mid = activation(mm(wmid_ref[...], h_in) + b_mid)
        h_mid = h_mid.astype(bf16)
        h_mid_s[:, cols] = h_mid
        tend_s[:, cols] = mm(wout_s[...], h_mid).astype(bf16)
        d_mid = (bm_s[:, cols] * slope_mid).astype(bf16)
        d_mid_s[:, cols] = d_mid
        wide = d_mid.astype(f32)
        gbm[...] += wide[:, :128] + wide[:, 128:]
        return 0

    lax.fori_loop(0, 3, chunk, 0)
    tend_send[...] = tend_s[...].reshape(N_LEV, PAD, NLON)
    norm = 1.0 / math.sqrt(256 * NLON)

    def packed(value):
        return (value * norm).astype(bf16).reshape(N_LAT, 16, value.shape[1])

    bias = jnp.sum(gbm[...], axis=1, keepdims=True)
    gout = mm_nt(h_mid_s[...], up_s[...])
    send0[...] = packed(jnp.where(iota((512, 128), 1) == USED, bias, gout))
    wait_part0 = to_lat(lambda p: send0.at[p], part0)
    wait_tend = to_lev(lambda p: tend_send.at[p], tend_in)
    part0[lat] = send0[lat]
    tend_in[lev] = tend_send[lev]
    send1[...] = packed(mm_nt(d_mid_s[...], h_in_s[0:256, :]))
    wait_part1 = to_lat(lambda p: send1.at[p], part1)
    part1[lat] = send1[lat]
    send2[...] = packed(mm_nt(d_mid_s[...], h_in_s[256:512, :]))
    wait_part2 = to_lat(lambda p: send2.at[p], part2)
    part2[lat] = send2[lat]

    def delta_chunk(c, _):
        cols = columns(c)
        d_in_s[:, cols] = (mm(wmidT_s[...], d_mid_s[:, cols]) * slope_s[:, cols]).astype(bf16)
        return 0

    lax.fori_loop(0, 3, delta_chunk, 0)
    send3[...] = packed(mm_nt(d_in_s[...], in_s[...]))
    wait_part3 = to_lat(lambda p: send3.at[p], part3)
    part3[lat] = send3[lat]

    waits = []
    for wait, part, piece, pieces in (
        (wait_part0, part0, piece0, pieces0), (wait_part1, part1, piece1, pieces1),
        (wait_part2, part2, piece2, pieces2), (wait_part3, part3, piece3, pieces3),
    ):
        wait()
        piece[...] = total_of(part).astype(bf16)
        waits.append(to_lev(lambda p, piece=piece: piece, pieces))
        pieces[lev] = piece[...]
    finals = []
    for wait, pieces, done, tot in zip(
        waits, (pieces0, pieces1, pieces2, pieces3), (done0, done1, done2, done3),
        (tot0, tot1, tot2, tot3),
    ):
        wait()
        done[...] = total_of(pieces).astype(bf16)
        finals.append(to_lat(lambda p, done=done: done, tot))
        tot[lat] = done[...]
    wait_tend()
    for a in range(ROWS):
        piece = tend_in[a].astype(f32)
        for c in range(NLON // 128):
            at = pl.ds(96 * c + a, USED, stride=ROWS)
            turn[at, :] = turn[at, :] + piece[:USED, 128 * c : 128 * (c + 1)]
    for c in range(NLON // 128):
        state_ref[:, 128 * c : 128 * (c + 1)] = turn[96 * c : 96 * (c + 1), :]
    for wait in finals:
        wait()


def finish_kernel(tot0, tot1, tot2, tot3, gin_ref, gbin_ref, gmid_ref, gbmid_ref, gout_ref):
    last, first = tot0[...].reshape(512, 128), tot3[...].reshape(512, 128)
    gin_ref[...] = mm(first, feature_onehot((128, 96), 1))
    gout_ref[...] = mm_nt(feature_onehot((96, 128), 0), last)
    gmid_ref[:, :256] = tot1[...].reshape(512, 256).astype(f32)
    gmid_ref[:, 256:] = tot2[...].reshape(512, 256).astype(f32)
    pick = (iota((8, 128), 1) == USED).astype(f32).astype(bf16)
    gbin_ref[...] = mm_nt(pick, first)[:1]
    gbmid_ref[...] = mm_nt(pick, last)[:1]


def like(shape, dtype):
    return jax.ShapeDtypeStruct(shape, dtype)


def sems(count):
    return [pltpu.SemaphoreType.DMA((count,)), pltpu.SemaphoreType.DMA((count,))]


def on_device(
    prognostic, cotangent, damping, in_scale, w_in, b_in, w_mid, b_mid, w_out, wave_order, lat_order
):
    high, low = dft_tables()
    order = wave_order.reshape(1, TRUNC)
    lats = lat_order.reshape(1, 256)
    count = ROWS * USED
    waves16 = pltpu.VMEM((N_LAT, PAD, 128), bf16)
    waves32 = pltpu.VMEM((N_LAT, PAD, 128), f32)
    blocks = pltpu.VMEM((N_LEV, PAD, NLON), bf16)
    wide16 = pltpu.VMEM((512, NLON), bf16)
    wide32 = pltpu.VMEM((512, NLON), f32)
    skinny = pltpu.VMEM((128, NLON), bf16)
    widths = (128, 256, 256, 128)

    def per_piece(*leading):
        return [pltpu.VMEM((*leading, 16, width), bf16) for width in widths]

    scratch = [
        pltpu.VMEM((576, 128), f32), pltpu.VMEM((128, NLON), f32), waves32, blocks, blocks,
        waves16, waves16, pltpu.VMEM((2 * HALF, 128), f32), waves32, waves32,
        pltpu.VMEM((576, 128), f32), blocks, blocks,
        pltpu.VMEM((512, 128), bf16), pltpu.VMEM((128, 512), bf16), pltpu.VMEM((512, 128), bf16),
        pltpu.VMEM((512, 512), bf16), pltpu.VMEM((512, 128), f32), pltpu.VMEM((512, 128), f32),
        skinny, skinny, wide32, wide16, wide32, wide16, wide16, wide16,
        pltpu.VMEM((512, 128), f32), skinny, blocks, blocks,
        *per_piece(N_LAT), *per_piece(N_LAT), *per_piece(), *per_piece(N_LEV), *per_piece(),
    ]
    lat_sems, lev_sems = sems(N_LAT), sems(N_LEV)
    scratch += lat_sems + lev_sems + lat_sems + lev_sems
    scratch += lat_sems + lev_sems + lat_sems * 3
    scratch += lev_sems * 4 + lat_sems * 4
    spectral, state, *totals = pl.pallas_call(
        step_kernel,
        out_shape=[
            like((WAVES, 2, 4, 3, TRUNC), f32), like((count, NLON), f32),
            *[like((N_LAT, 16, width), bf16) for width in widths],
        ],
        in_specs=[VMEM] * 7 + [SMEM] * 3 + [VMEM] * 5,
        out_specs=[VMEM] * 6,
        scratch_shapes=scratch,
        compiler_params=pltpu.CompilerParams(collective_id=0, has_side_effects=True),
        name="step",
    )(
        prognostic.reshape(count, NLON), cotangent.reshape(count, NLON), high, low, order, lats,
        diagonal_table(), degree_table(), damping, in_scale,
        w_in, b_in.reshape(1, 512), w_mid, b_mid.reshape(1, 512), w_out,
    )
    gin, gbin, gmid, gbmid, gout = pl.pallas_call(
        finish_kernel,
        out_shape=[
            like((512, 96), f32), like((1, 512), f32), like((512, 512), f32), like((1, 512), f32),
            like((96, 512), f32),
        ],
        in_specs=[VMEM] * 4,
        out_specs=[VMEM] * 5,
        name="finish",
    )(*totals)
    return (
        state.reshape(prognostic.shape), spectral, gin, gbin.reshape(512), gmid, gbmid.reshape(512), gout,
    )


def solution(mesh):
    return jax.shard_map(
        on_device,
        mesh=mesh,
        in_specs=(
            P(None, "lev", "lat", None),
            P(None, "lev", "lat", None),
            P(None, "lev"),
            P(),
            P(),
            P(),
            P(),
            P(),
            P(),
            P(),
            P(),
        ),
        out_specs=(
            P(None, "lev", "lat", None),
            P("lat", None, None, "lev", None),
            P(),
            P(),
            P(),
            P(),
            P(),
        ),
        check_vma=False,
    )
```

```python
import math

import jax
import jax.numpy as jnp
import numpy as np
from jax import lax
from jax.experimental import pallas as pl
from jax.experimental.pallas import tpu as pltpu
from jax.sharding import PartitionSpec as P

f32 = jnp.float32
bf16 = jnp.bfloat16

TRUNC = 256
NLON = 768
N_LAT = 32
N_LEV = 8
WAVES = 8
ROWS = 8
PAD = 16
USED = 12
HALF = TRUNC * WAVES
SCALE_BITS = 110
MESH = pl.DeviceIdType.MESH
VMEM = pl.BlockSpec(memory_space=pltpu.VMEM)
SMEM = pl.BlockSpec(memory_space=pltpu.SMEM)


def dft_tables():
    n = np.arange(NLON)[:, None]
    m = np.arange(TRUNC)[None, :]
    angle = 2.0 * np.pi * ((n * m) % NLON) / NLON
    table = np.concatenate([np.cos(angle), -np.sin(angle)], axis=1)
    high = table.astype(jnp.bfloat16)
    low = (table - high.astype(np.float64)).astype(jnp.bfloat16)
    return jnp.asarray(high), jnp.asarray(low)


def diagonal_table():
    index = np.arange(1, TRUNC, dtype=np.float64)
    ratios = 0.5 * np.log((2.0 * index + 1.0) / (2.0 * index))
    totals = np.concatenate([[0.0], np.cumsum(ratios)]) - 0.5 * np.log(2.0)
    return jnp.asarray(totals.astype(np.float32)[None, :])


def degree_table():
    degree = np.arange(TRUNC, dtype=np.float64)
    root = np.sqrt(np.maximum(4.0 * degree * degree - 1.0, 0.0))
    before = np.concatenate([[1.0], np.maximum(root[:-1], 1.0)])
    return jnp.asarray(np.stack([root, 1.0 / before]).astype(np.float32))


def iota(shape, axis):
    return lax.broadcasted_iota(jnp.int32, shape, axis)


def mm(a, b):
    return lax.dot_general(a, b, (((1,), (0,)), ((), ())), preferred_element_type=f32)


def mm_nt(a, b):
    return lax.dot_general(a, b, (((1,), (1,)), ((), ())), preferred_element_type=f32)


def split(value):
    high = value.astype(bf16)
    return high, (value - high.astype(f32)).astype(bf16)


def wave_onehot(order_ref):
    return (iota((TRUNC, TRUNC), 0) == order_ref[...]).astype(f32).astype(bf16)


def feature_of(column):
    lev, pair = column // PAD, column % PAD
    feature = (pair % 4) * 24 + lev * 3 + pair // 4
    return jnp.where(pair < USED, feature, -1)


def feature_onehot(shape, feature_axis):
    column = feature_of(iota(shape, 1 - feature_axis))
    return (iota(shape, feature_axis) == column).astype(f32).astype(bf16)


def stored(i):
    return (i % 4) * 3 + i // 4


def take_rows(rows, source, target):
    for c in range(NLON // 128):
        value = source[:, 128 * c : 128 * (c + 1)].astype(f32)
        for i in range(USED):
            at = 96 * c + ROWS * i
            rows[at : at + ROWS, :] = value[ROWS * stored(i) : ROWS * (stored(i) + 1), :]
        for a in range(ROWS):
            picked = rows[pl.ds(96 * c + a, USED, stride=ROWS), :]
            target[PAD * a : PAD * a + USED, 128 * c : 128 * (c + 1)] = picked


def forward(x_ref, high_ref, low_ref, order_ref, lat_ref, rows, xs, fs, four_ref, lat):
    take_rows(rows, x_ref, xs)
    xh, xl = split(xs[...])
    modes = mm(xh, high_ref[...]) + mm(xl, high_ref[...]) + mm(xh, low_ref[...])
    theta = (math.pi / 256.0) * (lat_ref[...].astype(f32) + 0.5)
    weight = (math.pi / 256.0 / NLON) * jnp.sin(theta)
    row = iota((ROWS * PAD, 256), 0) // PAD + lat * ROWS
    picked = jnp.where(iota((ROWS * PAD, 256), 1) == row, weight, 0.0)
    modes = (modes * jnp.sum(picked, axis=1, keepdims=True)).astype(bf16)
    onehot = wave_onehot(order_ref)
    for k in range(2):
        ordered = mm(modes[:, k * 256 : (k + 1) * 256], onehot)
        fs[:, 8 * k : 8 * (k + 1), :] = ordered.T.reshape(N_LAT, 8, 128)
    four_ref[...] = fs[...].astype(bf16)


def legendre_table(order_ref, lat_ref, diag_ref, deg_ref, table, lat):
    lane = iota((WAVES, 256), 1)
    mine = lane == lat * WAVES + iota((WAVES, 256), 0)
    order = order_ref[...].astype(f32)
    wave = jnp.sum(jnp.where(mine, order, 0.0), axis=1, keepdims=True)
    diag_log = jnp.sum(
        jnp.where(lane.astype(f32) == wave, diag_ref[...], 0.0), axis=1, keepdims=True
    )
    source = (iota((256, 256), 1) % N_LAT) * ROWS + iota((256, 256), 1) // N_LAT
    reorder = (iota((256, 256), 0) == source).astype(f32).astype(bf16)
    lat_row = jnp.broadcast_to(lat_ref[...].astype(f32), (8, 256)).astype(bf16)
    theta = (math.pi / 256.0) * (mm(lat_row, reorder) + 0.5)
    cosine = jnp.cos(theta)
    start = jnp.exp(diag_log + wave * jnp.log(jnp.sin(theta)) + SCALE_BITS * math.log(2.0))
    wave128 = jnp.broadcast_to(wave, (WAVES, 128))
    square = wave128 * wave128
    descale = 2.0**-SCALE_BITS

    def step(degree, carried):
        latest, before, root_before = carried
        value = degree.astype(f32)
        gap = value * value - square
        safe = jnp.maximum(gap, 1.0)
        inverse = lax.rsqrt(safe)
        inverse = inverse * (1.5 - 0.5 * safe * inverse * inverse)
        root = jnp.maximum(gap, 0.0) * inverse
        upper = inverse * deg_ref[0, degree]
        lower = upper * root_before * deg_ref[1, degree]
        upper2 = jnp.concatenate([upper, upper], axis=1)
        lower2 = jnp.concatenate([lower, lower], axis=1)
        first = jnp.where(wave == value, start, 0.0)
        newest = (upper2 * cosine) * latest + (first - lower2 * before)
        scaled = newest * descale
        at = pl.multiple_of(degree * WAVES, WAVES)
        table[pl.ds(at, WAVES), :] = scaled[:, :128]
        table[pl.ds(at + HALF, WAVES), :] = scaled[:, 128:]
        return newest, latest, root

    table[0:WAVES, :] = jnp.zeros((WAVES, 128), f32)
    half = table[0:WAVES, :]
    zero = jnp.concatenate([half, half], axis=1)
    lax.fori_loop(0, TRUNC, step, (zero, zero, half), unroll=8)


def analysis(four_ref, damp_ref, spec_ref, table, rs, so):
    pair = iota((PAD, 256), 0)
    damping = jnp.zeros((PAD, 256), f32)
    for i in range(USED):
        damping = jnp.where(pair == i, damp_ref[i % 4, i // 4], damping)
    degree = iota((PAD, 256), 1).astype(f32)
    ratio = degree * (degree + 1.0) * (1.0 / (TRUNC * (TRUNC - 1.0)))
    response = 1.0 / (1.0 + damping * ratio * ratio)
    response = jnp.concatenate([response, response], axis=0)

    for i in range(N_LAT):
        rs[i] = four_ref[i].astype(f32)
    flat = rs.reshape(N_LAT * PAD, 128)
    turned = []
    for q in range(4):
        block = jnp.concatenate(
            [flat[pl.ds(4 * q + i, N_LAT, stride=PAD), :] for i in range(4)], axis=0
        )
        turned.append(block.T)

    def rows_of(kj):
        piece = turned[kj // 4]
        low = 32 * (kj % 4)
        return jnp.concatenate(
            [piece[PAD * a : PAD * (a + 1), low : low + 32] for a in range(ROWS)], axis=1
        )

    made = [None] * 16
    for j in range(WAVES):
        field = jnp.concatenate([rows_of(j), rows_of(8 + j)], axis=0).astype(bf16)
        left = table[pl.ds(j, TRUNC, stride=WAVES), :]
        right = table[pl.ds(HALF + j, TRUNC, stride=WAVES), :]
        high, low = split(jnp.concatenate([left, right], axis=1))
        coeffs = (mm_nt(field, high) + mm_nt(field, low)) * response
        for k in range(2):
            for e in range(3):
                at = PAD * k + 4 * e
                spec_ref[j, k, e] = coeffs[at : at + 4, :]
        ch, cl = split(coeffs)
        grid = mm(ch, high) + mm(cl, high) + mm(ch, low)
        made[j] = grid[:PAD]
        made[8 + j] = grid[PAD:]
    flat_out = so.reshape(N_LAT * PAD, 128)
    for q in range(4):
        block = jnp.concatenate(
            [
                jnp.concatenate(
                    [made[4 * q + i][:, 32 * a : 32 * (a + 1)] for i in range(4)], axis=1
                )
                for a in range(ROWS)
            ],
            axis=0,
        )
        back = block.T
        for i in range(4):
            flat_out[pl.ds(4 * q + i, N_LAT, stride=PAD), :] = back[32 * i : 32 * (i + 1)]


def mode_rows(syn_ref, order_ref, mh_s, ml_s):
    onehot = wave_onehot(order_ref)
    factor = jnp.where(iota((TRUNC, 128), 0) == 0, 1.0, 2.0)
    for k in range(2):
        part_high, part_low = split(syn_ref[:, 8 * k : 8 * (k + 1), :].reshape(TRUNC, 128))
        part = ((mm(onehot, part_high) + mm(onehot, part_low)) * factor).T
        mh_s[:, 256 * k : 256 * (k + 1)], ml_s[:, 256 * k : 256 * (k + 1)] = split(part)


def inverse(mh_s, ml_s, high_ref, low_ref, scale, in_ref, turn, chunk):
    points = slice(256 * chunk, 256 * (chunk + 1))
    high = high_ref[points, :]
    rows = mm_nt(mh_s[...], high) + mm_nt(ml_s[...], high) + mm_nt(mh_s[...], low_ref[points, :])
    for a in range(ROWS):
        piece = rows[PAD * a : PAD * (a + 1), :]
        in_ref[a] = (piece * scale).astype(bf16)
        for half in range(2):
            at = pl.ds(96 * (2 * chunk + half) + a, USED, stride=ROWS)
            turn[at, :] = piece[:USED, 128 * half : 128 * (half + 1)]


def prepare(win_ref, bin_ref, wmid_ref, bmid_ref, wout_ref, win_s, wout_s, woutT_s, wmidT_s, bin_s, bmid_s):
    win_s[...] = mm(feature_onehot((128, 96), 1), win_ref[...]).T.astype(bf16)
    wout = mm(feature_onehot((128, 96), 1), wout_ref[...])
    wout_s[...] = wout.astype(bf16)
    woutT_s[...] = wout.T.astype(bf16)
    wmidT_s[...] = wmid_ref[...].astype(f32).T.astype(bf16)
    bin_s[...] = jnp.broadcast_to(bin_ref[...], (128, 512)).T
    bmid_s[...] = jnp.broadcast_to(bmid_ref[...], (128, 512)).T


def activation(value):
    z = 0.5 + 0.5 * jnp.tanh(0.5 * value)
    return value * z, z * (1.0 + value * (1.0 - z))


def columns(c):
    return pl.ds(pl.multiple_of(c * 256, 256), 256)


def greet(axes):
    barrier = pltpu.get_barrier_semaphore()
    for axis, size in axes:
        me = lax.axis_index(axis)

        def signal(d, _):
            peer = lax.rem(me + d, size)
            pl.semaphore_signal(barrier, inc=1, device_id={axis: peer}, device_id_type=MESH)
            return 0

        lax.fori_loop(1, size, signal, 0)
    return lambda: pl.semaphore_wait(barrier, sum(size - 1 for _, size in axes))


def scatter(axis, size, source, landing, send, recv, stride=1):
    me = lax.axis_index(axis)

    def copy(d):
        peer = lax.rem(me + d * stride, size)
        return pltpu.make_async_remote_copy(
            src_ref=source(peer), dst_ref=landing, send_sem=send.at[d],
            recv_sem=recv.at[d], device_id={axis: peer}, device_id_type=MESH,
        )

    def start(d, _):
        copy(d).start()
        return 0

    def wait(d, _):
        copy(d).wait()
        return 0

    lax.fori_loop(1, size // stride, start, 0)
    return lambda: lax.fori_loop(1, size // stride, wait, 0)


def total_of(ref):
    def body(i, acc):
        return acc + ref[i].astype(f32)

    return lax.fori_loop(1, ref.shape[0], body, ref[0].astype(f32))


def step_kernel(
    x_ref, ct_ref, high_ref, low_ref, order_ref, lat_ref, diag_ref, deg_ref, damp_ref, scale_ref,
    win_ref, bin_ref, wmid_ref, bmid_ref, wout_ref,
    spec_ref, state_ref, tot0, tot1, tot2,
    rows, xs, fs, up_send, up_in, four_send, four_in, table, so, syn_in, turn, mh_s, ml_s,
    in_send0, in_send1, in_send2, in_in0, in_in1, in_in2,
    win_s, wout_s, woutT_s, wmidT_s, bin_s, bmid_s, in_s, up_s, bm_s, h_in_s, slope_s, h_mid_s,
    d_mid_s, d_in_s, gbm, tend_s, tend_send, tend_in,
    send0, send1, send2, pair0, pair1, pair2, sum0, sum1, sum2, part0, part1, part2,
    piece0, piece1, piece2, pieces0, pieces1, pieces2, done0, done1, done2,
    *semaphores,
):
    lat, lev = lax.axis_index("lat"), lax.axis_index("lev")
    core, column = lax.rem(lev, 2), lev // 2
    pairs = iter([semaphores[i : i + 2] for i in range(0, len(semaphores), 2)])
    met = greet((("lat", N_LAT), ("lev", N_LEV)))

    def to_lat(source, landing):
        return scatter("lat", N_LAT, source, landing, *next(pairs))

    def to_lev(source, landing, stride=1):
        return scatter("lev", N_LEV, source, landing, *next(pairs), stride=stride)

    def to_partner(source, landing):
        send, recv = next(pairs)
        copy = pltpu.make_async_remote_copy(
            src_ref=source, dst_ref=landing, send_sem=send.at[0], recv_sem=recv.at[0],
            device_id={"lev": lev + 1 - 2 * core}, device_id_type=MESH,
        )
        copy.start()
        return copy.wait

    xs[...] = jnp.zeros_like(xs)
    take_rows(rows, ct_ref, xs)
    for a in range(ROWS):
        up_send[a] = xs[PAD * a : PAD * (a + 1), :].astype(bf16)
    forward(x_ref, high_ref, low_ref, order_ref, lat_ref, rows, xs, fs, four_send, lat)
    met()
    wait_four = to_lat(lambda p: four_send.at[p], four_in.at[lat])
    wait_up = to_lev(lambda p: up_send.at[p], up_in.at[lev])
    four_in[lat] = four_send[lat]
    up_in[lev] = up_send[lev]
    legendre_table(order_ref, lat_ref, diag_ref, deg_ref, table, lat)
    wait_four()
    analysis(four_in, damp_ref, spec_ref, table, fs, so)
    wait_syn = to_lat(lambda p: so.at[p], syn_in.at[lat])
    syn_in[lat] = so[lat]
    prepare(
        win_ref, bin_ref, wmid_ref, bmid_ref, wout_ref, win_s, wout_s, woutT_s, wmidT_s, bin_s, bmid_s
    )
    pair = iota((PAD, 256), 0)
    scale = jnp.zeros((PAD, 256), f32)
    for i in range(USED):
        scale = jnp.where(pair == i, scale_ref[i % 4, lev * 3 + i // 4], scale)
    gbm[...] = jnp.zeros_like(gbm)
    wait_syn()
    mode_rows(syn_in, order_ref, mh_s, ml_s)
    wait_ins = []
    for c, (in_send, in_in) in enumerate(
        ((in_send0, in_in0), (in_send1, in_in1), (in_send2, in_in2))
    ):
        inverse(mh_s, ml_s, high_ref, low_ref, scale, in_send, turn, c)
        wait_ins.append(to_lev(lambda p, in_send=in_send: in_send.at[p], in_in.at[lev]))
        in_in[lev] = in_send[lev]
    wait_up()
    up_s[...] = up_in[...].reshape(128, NLON)

    def back_chunk(c, _):
        bm_s[:, columns(c)] = mm(woutT_s[...], up_s[:, columns(c)])
        return 0

    lax.fori_loop(0, 3, back_chunk, 0)
    ones = iota((128, 256), 0) == USED
    for c, in_in in enumerate((in_in0, in_in1, in_in2)):
        cols = slice(256 * c, 256 * (c + 1))
        wait_ins[c]()
        inputs = in_in[...].reshape(128, 256)
        inputs = jnp.where(ones, 1.0, inputs.astype(f32)).astype(bf16)
        in_s[:, cols] = inputs
        b_in = jnp.concatenate([bin_s[...], bin_s[...]], axis=1)
        h_in, slope_in = activation(mm(win_s[...], inputs) + b_in)
        h_in = h_in.astype(bf16)
        h_in_s[:, cols] = h_in
        slope_s[:, cols] = slope_in
        b_mid = jnp.concatenate([bmid_s[...], bmid_s[...]], axis=1)
        h_mid, slope_mid = activation(mm(wmid_ref[...], h_in) + b_mid)
        h_mid = h_mid.astype(bf16)
        h_mid_s[:, cols] = h_mid
        tend_s[:, cols] = mm(wout_s[...], h_mid).astype(bf16)
        d_mid = (bm_s[:, cols] * slope_mid).astype(bf16)
        d_mid_s[:, cols] = d_mid
        wide = d_mid.astype(f32)
        gbm[...] += wide[:, :128] + wide[:, 128:]
    tend_send[...] = tend_s[...].reshape(N_LEV, PAD, NLON)
    norm = 1.0 / math.sqrt(256 * NLON)

    def packed(value):
        return (value * norm).astype(bf16).reshape(N_LAT, 16, 128)

    def offer(send, pair):
        return to_partner(send.at[1 - core], pair)

    def reduce_scatter(wait, send, pair, total, part):
        wait()
        total[...] = (send[core].astype(f32) + pair[...].astype(f32)).astype(bf16)
        part[lat] = total[lat]
        return to_lat(lambda p: total.at[p], part.at[lat])

    def mid_unit(send, at):
        chosen = jnp.concatenate([h_in_s[at : at + 128, :], h_in_s[at + 256 : at + 384, :]], axis=0)
        value = mm_nt(d_mid_s[...], chosen)
        send[0] = packed(value[:, :128])
        send[1] = packed(value[:, 128:])

    mid_unit(send0, 0)
    offered0 = offer(send0, pair0)
    mid_unit(send1, 128)
    offered1 = offer(send1, pair1)
    wait_tend = to_lev(lambda p: tend_send.at[p], tend_in.at[lev])
    tend_in[lev] = tend_send[lev]
    wait_part0 = reduce_scatter(offered0, send0, pair0, sum0, part0)

    def delta_chunk(c, _):
        cols = columns(c)
        d_in_s[:, cols] = (mm(wmidT_s[...], d_mid_s[:, cols]) * slope_s[:, cols]).astype(bf16)
        return 0

    lax.fori_loop(0, 3, delta_chunk, 0)
    bias = jnp.sum(gbm[...], axis=1, keepdims=True)
    gout = mm_nt(h_mid_s[...], up_s[...])
    send2[0] = packed(jnp.where(iota((512, 128), 1) == USED, bias, gout))
    send2[1] = packed(mm_nt(d_in_s[...], in_s[...]))
    offered2 = offer(send2, pair2)
    wait_part1 = reduce_scatter(offered1, send1, pair1, sum1, part1)
    wait_part2 = reduce_scatter(offered2, send2, pair2, sum2, part2)

    waits = []
    for wait, part, piece, pieces in (
        (wait_part0, part0, piece0, pieces0), (wait_part1, part1, piece1, pieces1),
        (wait_part2, part2, piece2, pieces2),
    ):
        wait()
        piece[...] = total_of(part)
        waits.append(to_lev(lambda p, piece=piece: piece, pieces.at[column], stride=2))
        pieces[column] = piece[...]
    gathers = []
    for wait, pieces, done, tot in zip(
        waits, (pieces0, pieces1, pieces2), (done0, done1, done2), (tot0, tot1, tot2)
    ):
        wait()
        done[...] = total_of(pieces).astype(bf16)
        gathers.append(to_lat(lambda p, done=done: done, tot.at[core, lat]))
        tot[core, lat] = done[...]
    wait_tend()
    for a in range(ROWS):
        piece = tend_in[a].astype(f32)
        for c in range(NLON // 128):
            at = pl.ds(96 * c + a, USED, stride=ROWS)
            turn[at, :] = turn[at, :] + piece[:USED, 128 * c : 128 * (c + 1)]
    for c in range(NLON // 128):
        for i in range(USED):
            at = 96 * c + ROWS * i
            state_ref[ROWS * stored(i) : ROWS * (stored(i) + 1), 128 * c : 128 * (c + 1)] = turn[
                at : at + ROWS, :
            ]
    handed = []
    for wait, tot in zip(gathers, (tot0, tot1, tot2)):
        wait()
        handed.append(to_partner(tot.at[core], tot.at[core]))
    for wait in handed:
        wait()


def finish_kernel(
    spec_in, state_in, tot0, tot1, tot2,
    spec_ref, state_ref, gin_ref, gbin_ref, gmid_ref, gbmid_ref, gout_ref,
):
    spec_ref[...] = spec_in[...]
    state_ref[...] = state_in[...]
    last, first = tot2[0].reshape(512, 128), tot2[1].reshape(512, 128)
    gin_ref[...] = mm_nt(feature_onehot((96, 128), 0), first)
    gout_ref[...] = mm_nt(feature_onehot((96, 128), 0), last)
    for unit, tot in enumerate((tot0, tot1)):
        for half in range(2):
            at = 128 * unit + 256 * half
            gmid_ref[:, at : at + 128] = tot[half].reshape(512, 128).astype(f32)
    pick = (iota((8, 128), 1) == USED).astype(f32).astype(bf16)
    gbin_ref[...] = mm_nt(pick, first)[:1]
    gbmid_ref[...] = mm_nt(pick, last)[:1]


def like(shape, dtype):
    return jax.ShapeDtypeStruct(shape, dtype)


def sems(count):
    return [pltpu.SemaphoreType.DMA((count,)), pltpu.SemaphoreType.DMA((count,))]


def on_device(
    prognostic, cotangent, damping, in_scale, w_in, b_in, w_mid, b_mid, w_out, wave_order, lat_order
):
    high, low = dft_tables()
    order = wave_order.reshape(1, TRUNC)
    lats = lat_order.reshape(1, 256)
    count = ROWS * USED
    waves16 = pltpu.VMEM((N_LAT, PAD, 128), bf16)
    waves32 = pltpu.VMEM((N_LAT, PAD, 128), f32)
    blocks = pltpu.VMEM((N_LEV, PAD, NLON), bf16)
    wide16 = pltpu.VMEM((512, NLON), bf16)
    wide32 = pltpu.VMEM((512, NLON), f32)
    skinny = pltpu.VMEM((128, NLON), bf16)
    chunk = pltpu.VMEM((N_LEV, PAD, 256), bf16)
    unit = pltpu.VMEM((N_LAT, 16, 128), bf16)
    scratch = [
        pltpu.VMEM((576, 128), f32), pltpu.VMEM((128, NLON), f32), waves32, blocks, blocks,
        waves16, waves16, pltpu.VMEM((2 * HALF, 128), f32), waves32, waves32,
        pltpu.VMEM((576, 128), f32), pltpu.VMEM((128, 512), bf16), pltpu.VMEM((128, 512), bf16),
        *[chunk] * 6,
        pltpu.VMEM((512, 128), bf16), pltpu.VMEM((128, 512), bf16), pltpu.VMEM((512, 128), bf16),
        pltpu.VMEM((512, 512), bf16), pltpu.VMEM((512, 128), f32), pltpu.VMEM((512, 128), f32),
        skinny, skinny, wide32, wide16, wide32, wide16, wide16, wide16,
        pltpu.VMEM((512, 128), f32), skinny, blocks, blocks,
        *[pltpu.VMEM((2, N_LAT, 16, 128), bf16)] * 3, *[unit] * 3, *[unit] * 3, *[unit] * 3,
        *[pltpu.VMEM((16, 128), f32)] * 3, *[pltpu.VMEM((4, 16, 128), f32)] * 3,
        *[pltpu.VMEM((16, 128), bf16)] * 3,
    ]
    lat_sems, lev_sems, one_sems = sems(N_LAT), sems(N_LEV), sems(1)
    scratch += lat_sems + lev_sems + lat_sems + lev_sems * 3
    scratch += one_sems * 2 + lev_sems + lat_sems
    scratch += one_sems + lat_sems * 2 + lev_sems * 3 + lat_sems * 3 + one_sems * 3
    spec_shape = like((WAVES, 2, 3, 4, TRUNC), f32)
    state_shape = like((count, NLON), f32)
    passed = pl.pallas_call(
        step_kernel,
        out_shape=[spec_shape, state_shape, *[like((2, N_LAT, 16, 128), bf16)] * 3],
        in_specs=[VMEM] * 7 + [SMEM] * 3 + [VMEM] * 5,
        out_specs=[VMEM] * 5,
        scratch_shapes=scratch,
        compiler_params=pltpu.CompilerParams(collective_id=0, has_side_effects=True),
        name="step",
    )(
        prognostic.reshape(count, NLON), cotangent.reshape(count, NLON), high, low, order, lats,
        diagonal_table(), degree_table(), damping, in_scale,
        w_in.T, b_in.reshape(1, 512), w_mid, b_mid.reshape(1, 512), w_out,
    )
    spectral, state, gin, gbin, gmid, gbmid, gout = pl.pallas_call(
        finish_kernel,
        out_shape=[
            spec_shape, state_shape,
            like((96, 512), f32), like((1, 512), f32), like((512, 512), f32), like((1, 512), f32),
            like((96, 512), f32),
        ],
        in_specs=[VMEM] * 5,
        out_specs=[VMEM] * 7,
        name="finish",
    )(*passed)
    spectral = jnp.swapaxes(spectral, 2, 3)
    return (
        state.reshape(prognostic.shape), spectral, gin.T, gbin.reshape(512), gmid, gbmid.reshape(512), gout,
    )


def solution(mesh):
    return jax.shard_map(
        on_device,
        mesh=mesh,
        in_specs=(
            P(None, "lev", "lat", None),
            P(None, "lev", "lat", None),
            P(None, "lev"),
            P(),
            P(),
            P(),
            P(),
            P(),
            P(),
            P(),
            P(),
        ),
        out_specs=(
            P(None, "lev", "lat", None),
            P("lat", None, None, "lev", None),
            P(),
            P(),
            P(),
            P(),
            P(),
        ),
        check_vma=False,
    )
```

```python
import math

import jax
import jax.numpy as jnp
import numpy as np
from jax import lax
from jax.experimental import pallas as pl
from jax.experimental.pallas import tpu as pltpu
from jax.sharding import PartitionSpec as P

f32 = jnp.float32
bf16 = jnp.bfloat16

TRUNC = 256
NLON = 768
N_LAT = 32
N_LEV = 8
WAVES = 8
ROWS = 8
PAD = 16
USED = 12
HALF = TRUNC * WAVES
SCALE_BITS = 110
MESH = pl.DeviceIdType.MESH
VMEM = pl.BlockSpec(memory_space=pltpu.VMEM)
FAR = pl.BlockSpec(memory_space=pl.ANY)
SMEM = pl.BlockSpec(memory_space=pltpu.SMEM)


def dft_tables():
    n = np.arange(NLON)[:, None]
    m = np.arange(TRUNC)[None, :]
    angle = 2.0 * np.pi * ((n * m) % NLON) / NLON
    table = np.concatenate([np.cos(angle), -np.sin(angle)], axis=1)
    high = table.astype(jnp.bfloat16)
    low = (table - high.astype(np.float64)).astype(jnp.bfloat16)
    return jnp.asarray(high), jnp.asarray(low)


def diagonal_table():
    index = np.arange(1, TRUNC, dtype=np.float64)
    ratios = 0.5 * np.log((2.0 * index + 1.0) / (2.0 * index))
    totals = np.concatenate([[0.0], np.cumsum(ratios)]) - 0.5 * np.log(2.0)
    return jnp.asarray(totals.astype(np.float32)[None, :])


def degree_table():
    degree = np.arange(TRUNC, dtype=np.float64)
    root = np.sqrt(np.maximum(4.0 * degree * degree - 1.0, 0.0))
    before = np.concatenate([[1.0], np.maximum(root[:-1], 1.0)])
    return jnp.asarray(np.stack([root, 1.0 / before]).astype(np.float32))


def iota(shape, axis):
    return lax.broadcasted_iota(jnp.int32, shape, axis)


def mm(a, b):
    return lax.dot_general(a, b, (((1,), (0,)), ((), ())), preferred_element_type=f32)


def mm_nt(a, b):
    return lax.dot_general(a, b, (((1,), (1,)), ((), ())), preferred_element_type=f32)


def split(value):
    high = value.astype(bf16)
    return high, (value - high.astype(f32)).astype(bf16)


def wave_onehot(order_ref):
    return (iota((TRUNC, TRUNC), 0) == order_ref[...]).astype(f32).astype(bf16)


def feature_of(column):
    lev, pair = column // PAD, column % PAD
    feature = (pair % 4) * 24 + lev * 3 + pair // 4
    return jnp.where(pair < USED, feature, -1)


def feature_onehot(shape, feature_axis):
    column = feature_of(iota(shape, 1 - feature_axis))
    return (iota(shape, feature_axis) == column).astype(f32).astype(bf16)


def stored(i):
    return (i % 4) * 3 + i // 4


def take_rows(rows, source, target):
    for c in range(NLON // 128):
        value = source[:, 128 * c : 128 * (c + 1)].astype(f32)
        for i in range(USED):
            at = 96 * c + ROWS * i
            rows[at : at + ROWS, :] = value[ROWS * stored(i) : ROWS * (stored(i) + 1), :]
        for a in range(ROWS):
            picked = rows[pl.ds(96 * c + a, USED, stride=ROWS), :]
            target[PAD * a : PAD * a + USED, 128 * c : 128 * (c + 1)] = picked


def forward(high_ref, low_ref, order_ref, lat_ref, onehot_s, xs, fs, four_ref, lat):
    xh, xl = split(xs[...])
    modes = mm(xh, high_ref[...]) + mm(xl, high_ref[...]) + mm(xh, low_ref[...])
    theta = (math.pi / 256.0) * (lat_ref[...].astype(f32) + 0.5)
    weight = (math.pi / 256.0 / NLON) * jnp.sin(theta)
    row = iota((ROWS * PAD, 256), 0) // PAD + lat * ROWS
    picked = jnp.where(iota((ROWS * PAD, 256), 1) == row, weight, 0.0)
    modes = (modes * jnp.sum(picked, axis=1, keepdims=True)).astype(bf16)
    onehot = wave_onehot(order_ref)
    onehot_s[...] = onehot
    for k in range(2):
        ordered = mm(modes[:, k * 256 : (k + 1) * 256], onehot)
        fs[:, 8 * k : 8 * (k + 1), :] = ordered.T.reshape(N_LAT, 8, 128)
    four_ref[...] = fs[...].astype(bf16)


def legendre_table(order_ref, lat_ref, diag_ref, deg_ref, table, lat):
    lane = iota((WAVES, 256), 1)
    mine = lane == lat * WAVES + iota((WAVES, 256), 0)
    order = order_ref[...].astype(f32)
    wave = jnp.sum(jnp.where(mine, order, 0.0), axis=1, keepdims=True)
    diag_log = jnp.sum(
        jnp.where(lane.astype(f32) == wave, diag_ref[...], 0.0), axis=1, keepdims=True
    )
    source = (iota((256, 256), 1) % N_LAT) * ROWS + iota((256, 256), 1) // N_LAT
    reorder = (iota((256, 256), 0) == source).astype(f32).astype(bf16)
    lat_row = jnp.broadcast_to(lat_ref[...].astype(f32), (8, 256)).astype(bf16)
    theta = (math.pi / 256.0) * (mm(lat_row, reorder) + 0.5)
    cosine = jnp.cos(theta)
    start = jnp.exp(diag_log + wave * jnp.log(jnp.sin(theta)) + SCALE_BITS * math.log(2.0))
    wave128 = jnp.broadcast_to(wave, (WAVES, 128))
    square = wave128 * wave128
    descale = 2.0**-SCALE_BITS

    def step(degree, carried):
        latest, before, root_before = carried
        value = degree.astype(f32)
        gap = value * value - square
        safe = jnp.maximum(gap, 1.0)
        inverse = lax.rsqrt(safe)
        inverse = inverse * (1.5 - 0.5 * safe * inverse * inverse)
        root = jnp.maximum(gap, 0.0) * inverse
        upper = inverse * deg_ref[0, degree]
        lower = upper * root_before * deg_ref[1, degree]
        upper2 = jnp.concatenate([upper, upper], axis=1)
        lower2 = jnp.concatenate([lower, lower], axis=1)
        first = jnp.where(wave == value, start, 0.0)
        newest = (upper2 * cosine) * latest + (first - lower2 * before)
        scaled = newest * descale
        at = pl.multiple_of(degree * WAVES, WAVES)
        table[pl.ds(at, WAVES), :] = scaled[:, :128]
        table[pl.ds(at + HALF, WAVES), :] = scaled[:, 128:]
        return newest, latest, root

    table[0:WAVES, :] = jnp.zeros((WAVES, 128), f32)
    half = table[0:WAVES, :]
    zero = jnp.concatenate([half, half], axis=1)
    lax.fori_loop(0, TRUNC, step, (zero, zero, half), unroll=8)


def split_table(table, highs, lows):
    for j in range(WAVES):
        left = table[pl.ds(j, TRUNC, stride=WAVES), :]
        right = table[pl.ds(HALF + j, TRUNC, stride=WAVES), :]
        highs[j], lows[j] = split(jnp.concatenate([left, right], axis=1))


def damp_response(damp_ref):
    pair = iota((PAD, 256), 0)
    damping = jnp.zeros((PAD, 256), f32)
    for i in range(USED):
        damping = jnp.where(pair == i, damp_ref[i % 4, i // 4], damping)
    degree = iota((PAD, 256), 1).astype(f32)
    ratio = degree * (degree + 1.0) * (1.0 / (TRUNC * (TRUNC - 1.0)))
    response = 1.0 / (1.0 + damping * ratio * ratio)
    return jnp.concatenate([response, response], axis=0)


def analysis(four_ref, response, spec_ref, highs, lows, rs, so):
    for i in range(N_LAT):
        rs[i] = four_ref[i].astype(f32)
    flat = rs.reshape(N_LAT * PAD, 128)
    turned = []
    for q in range(4):
        block = jnp.concatenate(
            [flat[pl.ds(4 * q + i, N_LAT, stride=PAD), :] for i in range(4)], axis=0
        )
        turned.append(block.T)

    def rows_of(kj):
        piece = turned[kj // 4]
        low = 32 * (kj % 4)
        return jnp.concatenate(
            [piece[PAD * a : PAD * (a + 1), low : low + 32] for a in range(ROWS)], axis=1
        )

    made = [None] * 16
    for j in range(WAVES):
        field = jnp.concatenate([rows_of(j), rows_of(8 + j)], axis=0).astype(bf16)
        high, low = highs[j], lows[j]
        coeffs = (mm_nt(field, high) + mm_nt(field, low)) * response
        for k in range(2):
            for e in range(3):
                at = PAD * k + 4 * e
                spec_ref[j, k, e] = coeffs[at : at + 4, :]
        ch, cl = split(coeffs)
        grid = mm(ch, high) + mm(cl, high) + mm(ch, low)
        made[j] = grid[:PAD]
        made[8 + j] = grid[PAD:]
    flat_out = so.reshape(N_LAT * PAD, 128)
    for q in range(4):
        block = jnp.concatenate(
            [
                jnp.concatenate(
                    [made[4 * q + i][:, 32 * a : 32 * (a + 1)] for i in range(4)], axis=1
                )
                for a in range(ROWS)
            ],
            axis=0,
        )
        back = block.T
        for i in range(4):
            flat_out[pl.ds(4 * q + i, N_LAT, stride=PAD), :] = back[32 * i : 32 * (i + 1)]


def inverse_table(high_ref, low_ref, order_ref, onehot_s, own_high, own_low):
    factor = jnp.where(order_ref[...] == 0, 1.0, 2.0)
    for source, target in ((high_ref, own_high), (low_ref, own_low)):
        for k in range(2):
            cols = slice(256 * k, 256 * (k + 1))
            target[:, cols] = (mm(source[:, cols], onehot_s[...]) * factor).astype(bf16)


def mode_rows(syn_ref, mh_s, ml_s):
    for k in range(2):
        part = syn_ref[:, 8 * k : 8 * (k + 1), :].reshape(TRUNC, 128).T
        mh_s[:, 256 * k : 256 * (k + 1)], ml_s[:, 256 * k : 256 * (k + 1)] = split(part)


def inverse(mh_s, ml_s, high_ref, low_ref, scale, in_ref, turn, chunk):
    points = slice(256 * chunk, 256 * (chunk + 1))
    high = high_ref[points, :]
    rows = mm_nt(mh_s[...], high) + mm_nt(ml_s[...], high) + mm_nt(mh_s[...], low_ref[points, :])
    for a in range(ROWS):
        piece = rows[PAD * a : PAD * (a + 1), :]
        in_ref[a] = (piece * scale).astype(bf16)
        for half in range(2):
            at = pl.ds(96 * (2 * chunk + half) + a, USED, stride=ROWS)
            turn[at, :] = piece[:USED, 128 * half : 128 * (half + 1)]


def prepare(win_ref, bin_ref, wmid_ref, bmid_ref, wout_ref, win_s, wout_s, woutT_s, wmidT_s, bin_s, bmid_s):
    win_s[...] = mm(feature_onehot((128, 96), 1), win_ref[...]).T.astype(bf16)
    wout = mm(feature_onehot((128, 96), 1), wout_ref[...])
    wout_s[...] = wout.astype(bf16)
    woutT_s[...] = wout.T.astype(bf16)
    wmidT_s[...] = wmid_ref[...].astype(f32).T.astype(bf16)
    bin_s[...] = jnp.broadcast_to(bin_ref[...], (128, 512)).T
    bmid_s[...] = jnp.broadcast_to(bmid_ref[...], (128, 512)).T


def activation(value):
    z = 0.5 + 0.5 * jnp.tanh(0.5 * value)
    return value * z, z * (1.0 + value * (1.0 - z))


def columns(c):
    return pl.ds(pl.multiple_of(c * 256, 256), 256)


def greet(axes):
    barrier = pltpu.get_barrier_semaphore()
    for axis, size in axes:
        me = lax.axis_index(axis)

        def signal(d, _):
            peer = lax.rem(me + d, size)
            pl.semaphore_signal(barrier, inc=1, device_id={axis: peer}, device_id_type=MESH)
            return 0

        lax.fori_loop(1, size, signal, 0)
    return lambda: pl.semaphore_wait(barrier, sum(size - 1 for _, size in axes))


def scatter(axis, size, source, landing, send, recv, stride=1):
    me = lax.axis_index(axis)

    def copy(d):
        peer = lax.rem(me + d * stride, size)
        return pltpu.make_async_remote_copy(
            src_ref=source(peer), dst_ref=landing, send_sem=send.at[d],
            recv_sem=recv.at[d], device_id={axis: peer}, device_id_type=MESH,
        )

    def start(d, _):
        copy(d).start()
        return 0

    def wait(d, _):
        copy(d).wait()
        return 0

    lax.fori_loop(1, size // stride, start, 0)
    return lambda: lax.fori_loop(1, size // stride, wait, 0)


def total_of(ref):
    def body(i, acc):
        return acc + ref[i].astype(f32)

    return lax.fori_loop(1, ref.shape[0], body, ref[0].astype(f32))


def step_kernel(
    x_far, ct_far, high_far, low_far, order_ref, lat_ref, diag_ref, deg_ref, damp_ref, scale_ref,
    win_far, bin_ref, wmid_far, bmid_ref, wout_far,
    spec_far, state_far, tot0_far, tot1_far,
    x_ref, ct_ref, high_ref, low_ref, win_ref, wmid_ref, wout_ref, spec_ref, state_ref, tot0, tot1,
    onehot_s, highs, lows, own_high, own_low, local_sem,
    rows, xs, fs, up_send, up_in, four_send, four_in, table, so, syn_in, turn, mh_s, ml_s,
    in_send0, in_send1, in_send2, in_in0, in_in1, in_in2,
    win_s, wout_s, woutT_s, wmidT_s, bin_s, bmid_s, in_s, up_s, bm_s, h_in_s, slope_s, h_mid_s,
    d_mid_s, d_in_s, gbm, tend_s, tend_send, tend_in,
    send0, send1, pair0, pair1, sum0, sum1, part0, part1,
    piece0, piece1, pieces0, pieces1, done0, done1,
    *semaphores,
):
    lat, lev = lax.axis_index("lat"), lax.axis_index("lev")
    core, column = lax.rem(lev, 2), lev // 2
    pairs = iter([semaphores[i : i + 2] for i in range(0, len(semaphores), 2)])
    met = greet((("lat", N_LAT), ("lev", N_LEV)))

    def to_lat(source, landing):
        return scatter("lat", N_LAT, source, landing, *next(pairs))

    def to_lev(source, landing, stride=1):
        return scatter("lev", N_LEV, source, landing, *next(pairs), stride=stride)

    def to_partner(source, landing):
        send, recv = next(pairs)
        copy = pltpu.make_async_remote_copy(
            src_ref=source, dst_ref=landing, send_sem=send.at[0], recv_sem=recv.at[0],
            device_id={"lev": lev + 1 - 2 * core}, device_id_type=MESH,
        )
        copy.start()
        return copy.wait

    moves = iter(range(16))

    def move(source, target):
        copy = pltpu.make_async_copy(source, target, local_sem.at[next(moves)])
        copy.start()
        return copy

    got_x = move(x_far, x_ref)
    got_high = move(high_far, high_ref)
    got_low = move(low_far, low_ref)
    got_ct = move(ct_far, ct_ref)
    got_weights = [move(win_far, win_ref), move(wout_far, wout_ref), move(wmid_far, wmid_ref)]
    xs[...] = jnp.zeros_like(xs)
    got_x.wait()
    take_rows(rows, x_ref, xs)
    got_high.wait()
    got_low.wait()
    forward(high_ref, low_ref, order_ref, lat_ref, onehot_s, xs, fs, four_send, lat)
    met()
    wait_four = to_lat(lambda p: four_send.at[p], four_in.at[lat])
    four_in[lat] = four_send[lat]
    got_ct.wait()
    take_rows(rows, ct_ref, xs)
    for a in range(ROWS):
        up_send[a] = xs[PAD * a : PAD * (a + 1), :].astype(bf16)
    up_in[lev] = up_send[lev]
    legendre_table(order_ref, lat_ref, diag_ref, deg_ref, table, lat)
    split_table(table, highs, lows)
    response = damp_response(damp_ref)
    wait_four()
    wait_up = to_lev(lambda p: up_send.at[p], up_in.at[lev])
    analysis(four_in, response, spec_ref, highs, lows, fs, so)
    wait_syn = to_lat(lambda p: so.at[p], syn_in.at[lat])
    syn_in[lat] = so[lat]
    put_spec = move(spec_ref, spec_far)
    inverse_table(high_ref, low_ref, order_ref, onehot_s, own_high, own_low)
    for got in got_weights:
        got.wait()
    prepare(
        win_ref, bin_ref, wmid_ref, bmid_ref, wout_ref, win_s, wout_s, woutT_s, wmidT_s, bin_s, bmid_s
    )
    pair = iota((PAD, 256), 0)
    scale = jnp.zeros((PAD, 256), f32)
    for i in range(USED):
        scale = jnp.where(pair == i, scale_ref[i % 4, lev * 3 + i // 4], scale)
    gbm[...] = jnp.zeros_like(gbm)
    wait_syn()
    mode_rows(syn_in, mh_s, ml_s)
    wait_ins = []
    for c, (in_send, in_in) in enumerate(
        ((in_send0, in_in0), (in_send1, in_in1), (in_send2, in_in2))
    ):
        inverse(mh_s, ml_s, own_high, own_low, scale, in_send, turn, c)
        wait_ins.append(to_lev(lambda p, in_send=in_send: in_send.at[p], in_in.at[lev]))
        in_in[lev] = in_send[lev]
    wait_up()
    up_s[...] = up_in[...].reshape(128, NLON)

    def back_chunk(c, _):
        bm_s[:, columns(c)] = mm(woutT_s[...], up_s[:, columns(c)])
        return 0

    lax.fori_loop(0, 3, back_chunk, 0)
    ones = iota((128, 256), 0) == USED
    for c, in_in in enumerate((in_in0, in_in1, in_in2)):
        cols = slice(256 * c, 256 * (c + 1))
        wait_ins[c]()
        inputs = in_in[...].reshape(128, 256)
        inputs = jnp.where(ones, 1.0, inputs.astype(f32)).astype(bf16)
        in_s[:, cols] = inputs
        b_in = jnp.concatenate([bin_s[...], bin_s[...]], axis=1)
        h_in, slope_in = activation(mm(win_s[...], inputs) + b_in)
        h_in = h_in.astype(bf16)
        h_in_s[:, cols] = h_in
        slope_s[:, cols] = slope_in
        b_mid = jnp.concatenate([bmid_s[...], bmid_s[...]], axis=1)
        h_mid, slope_mid = activation(mm(wmid_ref[...], h_in) + b_mid)
        h_mid = h_mid.astype(bf16)
        h_mid_s[:, cols] = h_mid
        tend_s[:, cols] = mm(wout_s[...], h_mid).astype(bf16)
        d_mid = (bm_s[:, cols] * slope_mid).astype(bf16)
        d_mid_s[:, cols] = d_mid
        wide = d_mid.astype(f32)
        gbm[...] += wide[:, :128] + wide[:, 128:]
    tend_send[...] = tend_s[...].reshape(N_LEV, PAD, NLON)
    norm = 1.0 / math.sqrt(256 * NLON)

    def packed(value):
        return (value * norm).astype(bf16).reshape(N_LAT, 16, value.shape[1])

    def offer(send, pair):
        return to_partner(send.at[1 - core], pair)

    def reduce_scatter(wait, send, pair, total, part):
        wait()
        total[...] = (send[core].astype(f32) + pair[...].astype(f32)).astype(bf16)
        part[lat] = total[lat]
        return to_lat(lambda p: total.at[p], part.at[lat])

    for half in range(2):
        send0[half] = packed(mm_nt(d_mid_s[...], h_in_s[256 * half : 256 * (half + 1), :]))
    offered0 = offer(send0, pair0)
    wait_tend = to_lev(lambda p: tend_send.at[p], tend_in.at[lev])
    tend_in[lev] = tend_send[lev]
    wait_part0 = reduce_scatter(offered0, send0, pair0, sum0, part0)

    def delta_chunk(c, _):
        cols = columns(c)
        d_in_s[:, cols] = (mm(wmidT_s[...], d_mid_s[:, cols]) * slope_s[:, cols]).astype(bf16)
        return 0

    lax.fori_loop(0, 3, delta_chunk, 0)
    bias = jnp.sum(gbm[...], axis=1, keepdims=True)
    gout = mm_nt(h_mid_s[...], up_s[...])
    send1[0] = packed(jnp.where(iota((512, 128), 1) == USED, bias, gout))
    send1[1] = packed(mm_nt(d_in_s[...], in_s[...]))
    offered1 = offer(send1, pair1)
    wait_part1 = reduce_scatter(offered1, send1, pair1, sum1, part1)

    waits = []
    for wait, part, piece, pieces in (
        (wait_part0, part0, piece0, pieces0), (wait_part1, part1, piece1, pieces1),
    ):
        wait()
        piece[...] = total_of(part)
        waits.append(to_lev(lambda p, piece=piece: piece, pieces.at[column], stride=2))
        pieces[column] = piece[...]
    gathers = []
    for wait, pieces, done, tot in zip(waits, (pieces0, pieces1), (done0, done1), (tot0, tot1)):
        wait()
        done[...] = total_of(pieces).astype(bf16)
        gathers.append(to_lat(lambda p, done=done: done, tot.at[core, lat]))
        tot[core, lat] = done[...]
    wait_tend()
    for a in range(ROWS):
        piece = tend_in[a].astype(f32)
        for c in range(NLON // 128):
            at = pl.ds(96 * c + a, USED, stride=ROWS)
            turn[at, :] = turn[at, :] + piece[:USED, 128 * c : 128 * (c + 1)]
    for c in range(NLON // 128):
        for i in range(USED):
            at = 96 * c + ROWS * i
            state_ref[ROWS * stored(i) : ROWS * (stored(i) + 1), 128 * c : 128 * (c + 1)] = turn[
                at : at + ROWS, :
            ]
    puts = [put_spec, move(state_ref, state_far)]
    handed = []
    totals = ((tot0, tot0_far), (tot1, tot1_far))
    for wait, (tot, tot_far) in zip(gathers, totals):
        wait()
        handed.append(to_partner(tot.at[core], tot.at[core]))
        puts.append(move(tot.at[core], tot_far.at[core]))
    for wait, (tot, tot_far) in zip(handed, totals):
        wait()
        puts.append(move(tot.at[1 - core], tot_far.at[1 - core]))
    for put in puts:
        put.wait()


def finish_kernel(
    spec_in, state_in, tot0, tot1,
    spec_ref, state_ref, gin_ref, gbin_ref, gmid_ref, gbmid_ref, gout_ref,
):
    spec_ref[...] = spec_in[...]
    state_ref[...] = state_in[...]
    last, first = tot1[0].reshape(512, 128), tot1[1].reshape(512, 128)
    gin_ref[...] = mm_nt(feature_onehot((96, 128), 0), first)
    gout_ref[...] = mm_nt(feature_onehot((96, 128), 0), last)
    for half in range(2):
        gmid_ref[:, 256 * half : 256 * (half + 1)] = tot0[half].reshape(512, 256).astype(f32)
    pick = (iota((8, 128), 1) == USED).astype(f32).astype(bf16)
    gbin_ref[...] = mm_nt(pick, first)[:1]
    gbmid_ref[...] = mm_nt(pick, last)[:1]


def like(shape, dtype):
    return jax.ShapeDtypeStruct(shape, dtype)


def sems(count):
    return [pltpu.SemaphoreType.DMA((count,)), pltpu.SemaphoreType.DMA((count,))]


def on_device(
    prognostic, cotangent, damping, in_scale, w_in, b_in, w_mid, b_mid, w_out, wave_order, lat_order
):
    high, low = dft_tables()
    order = wave_order.reshape(1, TRUNC)
    lats = lat_order.reshape(1, 256)
    count = ROWS * USED
    waves16 = pltpu.VMEM((N_LAT, PAD, 128), bf16)
    waves32 = pltpu.VMEM((N_LAT, PAD, 128), f32)
    blocks = pltpu.VMEM((N_LEV, PAD, NLON), bf16)
    wide16 = pltpu.VMEM((512, NLON), bf16)
    wide32 = pltpu.VMEM((512, NLON), f32)
    skinny = pltpu.VMEM((128, NLON), bf16)
    chunk = pltpu.VMEM((N_LEV, PAD, 256), bf16)
    widths = (256, 128)

    def per_unit(dtype, *leading):
        return [pltpu.VMEM((*leading, 16, width), dtype) for width in widths]

    spec_shape = like((WAVES, 2, 3, 4, TRUNC), f32)
    state_shape = like((count, NLON), f32)
    total_shapes = [like((2, N_LAT, 16, width), bf16) for width in widths]
    scratch = [
        pltpu.VMEM((count, NLON), f32), pltpu.VMEM((count, NLON), bf16),
        pltpu.VMEM((NLON, 512), bf16), pltpu.VMEM((NLON, 512), bf16),
        pltpu.VMEM((96, 512), bf16), pltpu.VMEM((512, 512), bf16), pltpu.VMEM((96, 512), bf16),
        pltpu.VMEM(spec_shape.shape, f32), pltpu.VMEM(state_shape.shape, f32),
        *per_unit(bf16, 2, N_LAT),
        pltpu.VMEM((TRUNC, TRUNC), bf16),
        pltpu.VMEM((WAVES, TRUNC, 256), bf16), pltpu.VMEM((WAVES, TRUNC, 256), bf16),
        pltpu.VMEM((NLON, 512), bf16), pltpu.VMEM((NLON, 512), bf16), pltpu.SemaphoreType.DMA((16,)),
        pltpu.VMEM((576, 128), f32), pltpu.VMEM((128, NLON), f32), waves32, blocks, blocks,
        waves16, waves16, pltpu.VMEM((2 * HALF, 128), f32), waves32, waves32,
        pltpu.VMEM((576, 128), f32), pltpu.VMEM((128, 512), bf16), pltpu.VMEM((128, 512), bf16),
        *[chunk] * 6,
        pltpu.VMEM((512, 128), bf16), pltpu.VMEM((128, 512), bf16), pltpu.VMEM((512, 128), bf16),
        pltpu.VMEM((512, 512), bf16), pltpu.VMEM((512, 128), f32), pltpu.VMEM((512, 128), f32),
        skinny, skinny, wide32, wide16, wide32, wide16, wide16, wide16,
        pltpu.VMEM((512, 128), f32), skinny, blocks, blocks,
        *per_unit(bf16, 2, N_LAT), *per_unit(bf16, N_LAT) * 3,
        *per_unit(f32), *per_unit(f32, 4), *per_unit(bf16),
    ]
    lat_sems, lev_sems, one_sems = sems(N_LAT), sems(N_LEV), sems(1)
    scratch += lat_sems + lev_sems + lat_sems + lev_sems * 3
    scratch += one_sems + lev_sems + lat_sems
    scratch += one_sems + lat_sems + lev_sems * 2 + lat_sems * 2 + one_sems * 2
    passed = pl.pallas_call(
        step_kernel,
        out_shape=[spec_shape, state_shape, *total_shapes],
        in_specs=[FAR] * 4 + [VMEM] * 3 + [SMEM] * 3 + [FAR, VMEM, FAR, VMEM, FAR],
        out_specs=[FAR] * 4,
        scratch_shapes=scratch,
        compiler_params=pltpu.CompilerParams(collective_id=0, has_side_effects=True),
        name="step",
    )(
        prognostic.reshape(count, NLON), cotangent.reshape(count, NLON), high, low, order, lats,
        diagonal_table(), degree_table(), damping, in_scale,
        w_in.T, b_in.reshape(1, 512), w_mid, b_mid.reshape(1, 512), w_out,
    )
    spectral, state, gin, gbin, gmid, gbmid, gout = pl.pallas_call(
        finish_kernel,
        out_shape=[
            spec_shape, state_shape,
            like((96, 512), f32), like((1, 512), f32), like((512, 512), f32), like((1, 512), f32),
            like((96, 512), f32),
        ],
        in_specs=[VMEM] * 4,
        out_specs=[VMEM] * 7,
        name="finish",
    )(*passed)
    spectral = jnp.swapaxes(spectral, 2, 3)
    return (
        state.reshape(prognostic.shape), spectral, gin.T, gbin.reshape(512), gmid, gbmid.reshape(512), gout,
    )


def solution(mesh):
    return jax.shard_map(
        on_device,
        mesh=mesh,
        in_specs=(
            P(None, "lev", "lat", None),
            P(None, "lev", "lat", None),
            P(None, "lev"),
            P(),
            P(),
            P(),
            P(),
            P(),
            P(),
            P(),
            P(),
        ),
        out_specs=(
            P(None, "lev", "lat", None),
            P("lat", None, None, "lev", None),
            P(),
            P(),
            P(),
            P(),
            P(),
        ),
        check_vma=False,
    )
```

```python
import math

import jax
import jax.numpy as jnp
import numpy as np
from jax import lax
from jax.experimental import pallas as pl
from jax.experimental.pallas import tpu as pltpu
from jax.sharding import PartitionSpec as P

f32 = jnp.float32
bf16 = jnp.bfloat16

TRUNC = 256
NLON = 768
N_LAT = 32
N_LEV = 8
WAVES = 8
ROWS = 8
PAD = 16
USED = 12
HALF = TRUNC * WAVES
SCALE_BITS = 110
MESH = pl.DeviceIdType.MESH
VMEM = pl.BlockSpec(memory_space=pltpu.VMEM)
FAR = pl.BlockSpec(memory_space=pl.ANY)
SMEM = pl.BlockSpec(memory_space=pltpu.SMEM)


def dft_tables():
    n = np.arange(NLON)[:, None]
    m = np.arange(TRUNC)[None, :]
    angle = 2.0 * np.pi * ((n * m) % NLON) / NLON
    table = np.concatenate([np.cos(angle), -np.sin(angle)], axis=1)
    high = table.astype(jnp.bfloat16)
    low = (table - high.astype(np.float64)).astype(jnp.bfloat16)
    return jnp.asarray(high), jnp.asarray(low)


def diagonal_table():
    index = np.arange(1, TRUNC, dtype=np.float64)
    ratios = 0.5 * np.log((2.0 * index + 1.0) / (2.0 * index))
    totals = np.concatenate([[0.0], np.cumsum(ratios)]) - 0.5 * np.log(2.0)
    return jnp.asarray(totals.astype(np.float32)[None, :])


def degree_table():
    degree = np.arange(TRUNC, dtype=np.float64)
    root = np.sqrt(np.maximum(4.0 * degree * degree - 1.0, 0.0))
    before = np.concatenate([[1.0], np.maximum(root[:-1], 1.0)])
    return jnp.asarray(np.stack([root, 1.0 / before]).astype(np.float32))


def iota(shape, axis):
    return lax.broadcasted_iota(jnp.int32, shape, axis)


def mm(a, b):
    return lax.dot_general(a, b, (((1,), (0,)), ((), ())), preferred_element_type=f32)


def mm_nt(a, b):
    return lax.dot_general(a, b, (((1,), (1,)), ((), ())), preferred_element_type=f32)


def split(value):
    high = value.astype(bf16)
    return high, (value - high.astype(f32)).astype(bf16)


def wave_onehot(order_ref):
    return (iota((TRUNC, TRUNC), 0) == order_ref[...]).astype(f32).astype(bf16)


def feature_of(column):
    lev, pair = column // PAD, column % PAD
    feature = (pair % 4) * 24 + lev * 3 + pair // 4
    return jnp.where(pair < USED, feature, -1)


def feature_onehot(shape, feature_axis):
    column = feature_of(iota(shape, 1 - feature_axis))
    return (iota(shape, feature_axis) == column).astype(f32).astype(bf16)


def stored(i):
    return (i % 4) * 3 + i // 4


def take_rows(rows, source, target):
    for c in range(NLON // 128):
        value = source[:, 128 * c : 128 * (c + 1)].astype(f32)
        for i in range(USED):
            at = 96 * c + ROWS * i
            rows[at : at + ROWS, :] = value[ROWS * stored(i) : ROWS * (stored(i) + 1), :]
        for a in range(ROWS):
            picked = rows[pl.ds(96 * c + a, USED, stride=ROWS), :]
            target[PAD * a : PAD * a + USED, 128 * c : 128 * (c + 1)] = picked


def forward(high_ref, low_ref, order_ref, lat_ref, onehot_s, xs, fs, four_ref, lat):
    xh, xl = split(xs[...])
    modes = mm(xh, high_ref[...]) + mm(xl, high_ref[...]) + mm(xh, low_ref[...])
    theta = (math.pi / 256.0) * (lat_ref[...].astype(f32) + 0.5)
    weight = (math.pi / 256.0 / NLON) * jnp.sin(theta)
    row = iota((ROWS * PAD, 256), 0) // PAD + lat * ROWS
    picked = jnp.where(iota((ROWS * PAD, 256), 1) == row, weight, 0.0)
    modes = (modes * jnp.sum(picked, axis=1, keepdims=True)).astype(bf16)
    onehot = wave_onehot(order_ref)
    onehot_s[...] = onehot
    for k in range(2):
        ordered = mm(modes[:, k * 256 : (k + 1) * 256], onehot)
        fs[:, 8 * k : 8 * (k + 1), :] = ordered.T.reshape(N_LAT, 8, 128)
    four_ref[...] = fs[...].astype(bf16)


def legendre_table(order_ref, lat_ref, diag_ref, deg_ref, table, lat):
    lane = iota((WAVES, 256), 1)
    mine = lane == lat * WAVES + iota((WAVES, 256), 0)
    order = order_ref[...].astype(f32)
    wave = jnp.sum(jnp.where(mine, order, 0.0), axis=1, keepdims=True)
    diag_log = jnp.sum(
        jnp.where(lane.astype(f32) == wave, diag_ref[...], 0.0), axis=1, keepdims=True
    )
    source = (iota((256, 256), 1) % N_LAT) * ROWS + iota((256, 256), 1) // N_LAT
    reorder = (iota((256, 256), 0) == source).astype(f32).astype(bf16)
    lat_row = jnp.broadcast_to(lat_ref[...].astype(f32), (8, 256)).astype(bf16)
    theta = (math.pi / 256.0) * (mm(lat_row, reorder) + 0.5)
    cosine = jnp.cos(theta)
    start = jnp.exp(diag_log + wave * jnp.log(jnp.sin(theta)) + SCALE_BITS * math.log(2.0))
    wave128 = jnp.broadcast_to(wave, (WAVES, 128))
    square = wave128 * wave128
    descale = 2.0**-SCALE_BITS

    def step(degree, carried):
        latest, before, root_before = carried
        value = degree.astype(f32)
        gap = value * value - square
        safe = jnp.maximum(gap, 1.0)
        inverse = lax.rsqrt(safe)
        inverse = inverse * (1.5 - 0.5 * safe * inverse * inverse)
        root = jnp.maximum(gap, 0.0) * inverse
        upper = inverse * deg_ref[0, degree]
        lower = upper * root_before * deg_ref[1, degree]
        upper2 = jnp.concatenate([upper, upper], axis=1)
        lower2 = jnp.concatenate([lower, lower], axis=1)
        first = jnp.where(wave == value, start, 0.0)
        newest = (upper2 * cosine) * latest + (first - lower2 * before)
        scaled = newest * descale
        at = pl.multiple_of(degree * WAVES, WAVES)
        table[pl.ds(at, WAVES), :] = scaled[:, :128]
        table[pl.ds(at + HALF, WAVES), :] = scaled[:, 128:]
        return newest, latest, root

    table[0:WAVES, :] = jnp.zeros((WAVES, 128), f32)
    half = table[0:WAVES, :]
    zero = jnp.concatenate([half, half], axis=1)
    lax.fori_loop(0, TRUNC, step, (zero, zero, half), unroll=8)


def split_table(table, highs, lows):
    for j in range(WAVES):
        left = table[pl.ds(j, TRUNC, stride=WAVES), :]
        right = table[pl.ds(HALF + j, TRUNC, stride=WAVES), :]
        highs[j], lows[j] = split(jnp.concatenate([left, right], axis=1))


def damp_response(damp_ref):
    pair = iota((PAD, 256), 0)
    damping = jnp.zeros((PAD, 256), f32)
    for i in range(USED):
        damping = jnp.where(pair == i, damp_ref[i % 4, i // 4], damping)
    degree = iota((PAD, 256), 1).astype(f32)
    ratio = degree * (degree + 1.0) * (1.0 / (TRUNC * (TRUNC - 1.0)))
    response = 1.0 / (1.0 + damping * ratio * ratio)
    return jnp.concatenate([response, response], axis=0)


def analysis(four_ref, response, spec_ref, highs, lows, rs, so):
    for i in range(N_LAT):
        rs[i] = four_ref[i].astype(f32)
    flat = rs.reshape(N_LAT * PAD, 128)
    turned = []
    for q in range(4):
        block = jnp.concatenate(
            [flat[pl.ds(4 * q + i, N_LAT, stride=PAD), :] for i in range(4)], axis=0
        )
        turned.append(block.T)

    def rows_of(kj):
        piece = turned[kj // 4]
        low = 32 * (kj % 4)
        return jnp.concatenate(
            [piece[PAD * a : PAD * (a + 1), low : low + 32] for a in range(ROWS)], axis=1
        )

    made = [None] * 16
    for j in range(WAVES):
        field = jnp.concatenate([rows_of(j), rows_of(8 + j)], axis=0).astype(bf16)
        high, low = highs[j], lows[j]
        coeffs = (mm_nt(field, high) + mm_nt(field, low)) * response
        for k in range(2):
            for e in range(3):
                at = PAD * k + 4 * e
                spec_ref[j, k, e] = coeffs[at : at + 4, :]
        ch, cl = split(coeffs)
        grid = mm(ch, high) + mm(cl, high) + mm(ch, low)
        made[j] = grid[:PAD]
        made[8 + j] = grid[PAD:]
    flat_out = so.reshape(N_LAT * PAD, 128)
    for q in range(4):
        block = jnp.concatenate(
            [
                jnp.concatenate(
                    [made[4 * q + i][:, 32 * a : 32 * (a + 1)] for i in range(4)], axis=1
                )
                for a in range(ROWS)
            ],
            axis=0,
        )
        back = block.T
        for i in range(4):
            flat_out[pl.ds(4 * q + i, N_LAT, stride=PAD), :] = back[32 * i : 32 * (i + 1)]


def inverse_table(high_ref, low_ref, order_ref, onehot_s, own_high, own_low):
    factor = jnp.where(order_ref[...] == 0, 1.0, 2.0)
    for source, target in ((high_ref, own_high), (low_ref, own_low)):
        for k in range(2):
            cols = slice(256 * k, 256 * (k + 1))
            target[:, cols] = (mm(source[:, cols], onehot_s[...]) * factor).astype(bf16)


def mode_rows(syn_ref, mh_s, ml_s):
    for k in range(2):
        part = syn_ref[:, 8 * k : 8 * (k + 1), :].reshape(TRUNC, 128).T
        mh_s[:, 256 * k : 256 * (k + 1)], ml_s[:, 256 * k : 256 * (k + 1)] = split(part)


def inverse(mh_s, ml_s, high_ref, low_ref, scale, in_ref, turn, chunk):
    points = slice(256 * chunk, 256 * (chunk + 1))
    high = high_ref[points, :]
    rows = mm_nt(mh_s[...], high) + mm_nt(ml_s[...], high) + mm_nt(mh_s[...], low_ref[points, :])
    for a in range(ROWS):
        piece = rows[PAD * a : PAD * (a + 1), :]
        in_ref[a] = (piece * scale).astype(bf16)
        for half in range(2):
            at = pl.ds(96 * (2 * chunk + half) + a, USED, stride=ROWS)
            turn[at, :] = piece[:USED, 128 * half : 128 * (half + 1)]


def prepare(win_ref, bin_ref, wmid_ref, bmid_ref, wout_ref, win_s, wout_s, woutT_s, wmidT_s, bin_s, bmid_s):
    win_s[...] = mm(feature_onehot((128, 96), 1), win_ref[...]).T.astype(bf16)
    wout = mm(feature_onehot((128, 96), 1), wout_ref[...])
    wout_s[...] = wout.astype(bf16)
    woutT_s[...] = wout.T.astype(bf16)
    wmidT_s[...] = wmid_ref[...].astype(f32).T.astype(bf16)
    bin_s[...] = jnp.broadcast_to(bin_ref[...], (128, 512)).T
    bmid_s[...] = jnp.broadcast_to(bmid_ref[...], (128, 512)).T


def activation(value):
    z = 0.5 + 0.5 * jnp.tanh(0.5 * value)
    return value * z, z * (1.0 + value * (1.0 - z))


def columns(c):
    return pl.ds(pl.multiple_of(c * 256, 256), 256)


def greet(axes):
    barrier = pltpu.get_barrier_semaphore()
    for axis, size in axes:
        me = lax.axis_index(axis)

        def signal(d, _):
            peer = lax.rem(me + d, size)
            pl.semaphore_signal(barrier, inc=1, device_id={axis: peer}, device_id_type=MESH)
            return 0

        lax.fori_loop(1, size, signal, 0)
    return lambda: pl.semaphore_wait(barrier, sum(size - 1 for _, size in axes))


def scatter(axis, size, source, landing, send, recv, stride=1):
    me = lax.axis_index(axis)

    def copy(d):
        peer = lax.rem(me + d * stride, size)
        return pltpu.make_async_remote_copy(
            src_ref=source(peer), dst_ref=landing, send_sem=send.at[d],
            recv_sem=recv.at[d], device_id={axis: peer}, device_id_type=MESH,
        )

    def start(d, _):
        copy(d).start()
        return 0

    def wait(d, _):
        copy(d).wait()
        return 0

    lax.fori_loop(1, size // stride, start, 0)
    return lambda: lax.fori_loop(1, size // stride, wait, 0)


def total_of(ref):
    def body(i, acc):
        return acc + ref[i].astype(f32)

    return lax.fori_loop(1, ref.shape[0], body, ref[0].astype(f32))


def step_kernel(
    x_far, ct_far, high_far, low_far, order_ref, lat_ref, diag_ref, deg_ref, damp_ref, scale_ref,
    win_far, bin_ref, wmid_far, bmid_ref, wout_far,
    spec_far, state_far, tot0_far, tot1_far,
    x_ref, ct_ref, high_ref, low_ref, win_ref, wmid_ref, wout_ref, spec_ref, state_ref, tot0, tot1,
    onehot_s, highs, lows, own_high, own_low, local_sem,
    rows, xs, fs, up_send, up_in, four_send, four_in, table, so, syn_in, turn, mh_s, ml_s,
    in_send0, in_send1, in_send2, in_in0, in_in1, in_in2,
    win_s, wout_s, woutT_s, wmidT_s, bin_s, bmid_s, in_s, up_s, bm_s, h_in_s, slope_s, h_mid_s,
    d_mid_s, d_in_s, gbm, tend_s, tend_send, tend_in,
    send0, send1, pair0, pair1, sum0, sum1, part0, part1,
    piece0, piece1, pieces0, pieces1, done0, done1,
    *semaphores,
):
    lat, lev = lax.axis_index("lat"), lax.axis_index("lev")
    core, column = lax.rem(lev, 2), lev // 2
    pairs = iter([semaphores[i : i + 2] for i in range(0, len(semaphores), 2)])
    met = greet((("lat", N_LAT), ("lev", N_LEV)))

    def to_lat(source, landing):
        return scatter("lat", N_LAT, source, landing, *next(pairs))

    def to_lev(source, landing, stride=1):
        return scatter("lev", N_LEV, source, landing, *next(pairs), stride=stride)

    def to_partner(source, landing):
        send, recv = next(pairs)
        copy = pltpu.make_async_remote_copy(
            src_ref=source, dst_ref=landing, send_sem=send.at[0], recv_sem=recv.at[0],
            device_id={"lev": lev + 1 - 2 * core}, device_id_type=MESH,
        )
        copy.start()
        return copy.wait

    moves = iter(range(16))

    def move(source, target):
        copy = pltpu.make_async_copy(source, target, local_sem.at[next(moves)])
        copy.start()
        return copy

    got_x = move(x_far, x_ref)
    got_high = move(high_far, high_ref)
    got_low = move(low_far, low_ref)
    got_ct = move(ct_far, ct_ref)
    got_weights = [move(win_far, win_ref), move(wout_far, wout_ref), move(wmid_far, wmid_ref)]
    xs[...] = jnp.zeros_like(xs)
    got_x.wait()
    take_rows(rows, x_ref, xs)
    got_high.wait()
    got_low.wait()
    forward(high_ref, low_ref, order_ref, lat_ref, onehot_s, xs, fs, four_send, lat)
    met()
    wait_four = to_lat(lambda p: four_send.at[p], four_in.at[lat])
    four_in[lat] = four_send[lat]
    got_ct.wait()
    take_rows(rows, ct_ref, xs)
    for a in range(ROWS):
        up_send[a] = xs[PAD * a : PAD * (a + 1), :].astype(bf16)
    up_in[lev] = up_send[lev]
    legendre_table(order_ref, lat_ref, diag_ref, deg_ref, table, lat)
    split_table(table, highs, lows)
    response = damp_response(damp_ref)
    wait_four()
    wait_up = to_lev(lambda p: up_send.at[p], up_in.at[lev])
    analysis(four_in, response, spec_ref, highs, lows, fs, so)
    wait_syn = to_lat(lambda p: so.at[p], syn_in.at[lat])
    syn_in[lat] = so[lat]
    put_spec = move(spec_ref, spec_far)
    inverse_table(high_ref, low_ref, order_ref, onehot_s, own_high, own_low)
    for got in got_weights:
        got.wait()
    prepare(
        win_ref, bin_ref, wmid_ref, bmid_ref, wout_ref, win_s, wout_s, woutT_s, wmidT_s, bin_s, bmid_s
    )
    pair = iota((PAD, 256), 0)
    scale = jnp.zeros((PAD, 256), f32)
    for i in range(USED):
        scale = jnp.where(pair == i, scale_ref[i % 4, lev * 3 + i // 4], scale)
    gbm[...] = jnp.zeros_like(gbm)
    wait_syn()
    mode_rows(syn_in, mh_s, ml_s)
    wait_ins = []
    for c, (in_send, in_in) in enumerate(
        ((in_send0, in_in0), (in_send1, in_in1), (in_send2, in_in2))
    ):
        inverse(mh_s, ml_s, own_high, own_low, scale, in_send, turn, c)
        wait_ins.append(to_lev(lambda p, in_send=in_send: in_send.at[p], in_in.at[lev]))
        in_in[lev] = in_send[lev]
    wait_up()
    up_s[...] = up_in[...].reshape(128, NLON)

    def back_chunk(c, _):
        bm_s[:, columns(c)] = mm(woutT_s[...], up_s[:, columns(c)])
        return 0

    lax.fori_loop(0, 3, back_chunk, 0)
    ones = iota((128, 256), 0) == USED
    for c, in_in in enumerate((in_in0, in_in1, in_in2)):
        cols = slice(256 * c, 256 * (c + 1))
        wait_ins[c]()
        inputs = in_in[...].reshape(128, 256)
        inputs = jnp.where(ones, 1.0, inputs.astype(f32)).astype(bf16)
        in_s[:, cols] = inputs
        b_in = jnp.concatenate([bin_s[...], bin_s[...]], axis=1)
        h_in, slope_in = activation(mm(win_s[...], inputs) + b_in)
        h_in = h_in.astype(bf16)
        h_in_s[:, cols] = h_in
        slope_s[:, cols] = slope_in
        b_mid = jnp.concatenate([bmid_s[...], bmid_s[...]], axis=1)
        h_mid, slope_mid = activation(mm(wmid_ref[...], h_in) + b_mid)
        h_mid = h_mid.astype(bf16)
        h_mid_s[:, cols] = h_mid
        tend_s[:, cols] = mm(wout_s[...], h_mid).astype(bf16)
        d_mid = (bm_s[:, cols] * slope_mid).astype(bf16)
        d_mid_s[:, cols] = d_mid
        wide = d_mid.astype(f32)
        gbm[...] += wide[:, :128] + wide[:, 128:]
    tend_send[...] = tend_s[...].reshape(N_LEV, PAD, NLON)
    norm = 1.0 / math.sqrt(256 * NLON)

    def packed(value):
        return (value * norm).astype(bf16).reshape(N_LAT, 16, value.shape[1])

    def offer(send, pair):
        return to_partner(send.at[1 - core], pair)

    def reduce_scatter(wait, send, pair, total, part):
        wait()
        total[...] = (send[core].astype(f32) + pair[...].astype(f32)).astype(bf16)
        part[lat] = total[lat]
        return to_lat(lambda p: total.at[p], part.at[lat])

    wait_tend = to_lev(lambda p: tend_send.at[p], tend_in.at[lev])
    tend_in[lev] = tend_send[lev]
    for half in range(2):
        send0[half] = packed(mm_nt(d_mid_s[...], h_in_s[256 * half : 256 * (half + 1), :]))
    offered0 = offer(send0, pair0)
    wait_part0 = reduce_scatter(offered0, send0, pair0, sum0, part0)

    def delta_chunk(c, _):
        cols = columns(c)
        d_in_s[:, cols] = (mm(wmidT_s[...], d_mid_s[:, cols]) * slope_s[:, cols]).astype(bf16)
        return 0

    lax.fori_loop(0, 3, delta_chunk, 0)
    bias = jnp.sum(gbm[...], axis=1, keepdims=True)
    gout = mm_nt(h_mid_s[...], up_s[...])
    send1[0] = packed(jnp.where(iota((512, 128), 1) == USED, bias, gout))
    send1[1] = packed(mm_nt(d_in_s[...], in_s[...]))
    offered1 = offer(send1, pair1)
    wait_part1 = reduce_scatter(offered1, send1, pair1, sum1, part1)

    waits = []
    for wait, part, piece, pieces in (
        (wait_part0, part0, piece0, pieces0), (wait_part1, part1, piece1, pieces1),
    ):
        wait()
        piece[...] = total_of(part)
        waits.append(to_lev(lambda p, piece=piece: piece, pieces.at[column], stride=2))
        pieces[column] = piece[...]
    gathers = []
    for wait, pieces, done, tot in zip(waits, (pieces0, pieces1), (done0, done1), (tot0, tot1)):
        wait()
        done[...] = total_of(pieces).astype(bf16)
        gathers.append(to_lat(lambda p, done=done: done, tot.at[core, lat]))
        tot[core, lat] = done[...]
    wait_tend()
    for a in range(ROWS):
        piece = tend_in[a].astype(f32)
        for c in range(NLON // 128):
            at = pl.ds(96 * c + a, USED, stride=ROWS)
            turn[at, :] = turn[at, :] + piece[:USED, 128 * c : 128 * (c + 1)]
    for c in range(NLON // 128):
        for i in range(USED):
            at = 96 * c + ROWS * i
            state_ref[ROWS * stored(i) : ROWS * (stored(i) + 1), 128 * c : 128 * (c + 1)] = turn[
                at : at + ROWS, :
            ]
    puts = [put_spec, move(state_ref, state_far)]
    handed = []
    totals = ((tot0, tot0_far), (tot1, tot1_far))
    for wait, (tot, tot_far) in zip(gathers, totals):
        wait()
        handed.append(to_partner(tot.at[core], tot.at[core]))
        puts.append(move(tot.at[core], tot_far.at[core]))
    for wait, (tot, tot_far) in zip(handed, totals):
        wait()
        puts.append(move(tot.at[1 - core], tot_far.at[1 - core]))
    for put in puts:
        put.wait()


def finish_kernel(
    spec_in, state_in, tot0, tot1,
    spec_ref, state_ref, gin_ref, gbin_ref, gmid_ref, gbmid_ref, gout_ref,
):
    spec_ref[...] = spec_in[...]
    state_ref[...] = state_in[...]
    last, first = tot1[0].reshape(512, 128), tot1[1].reshape(512, 128)
    gin_ref[...] = mm_nt(feature_onehot((96, 128), 0), first)
    gout_ref[...] = mm_nt(feature_onehot((96, 128), 0), last)
    for half in range(2):
        gmid_ref[:, 256 * half : 256 * (half + 1)] = tot0[half].reshape(512, 256).astype(f32)
    pick = (iota((8, 128), 1) == USED).astype(f32).astype(bf16)
    gbin_ref[...] = mm_nt(pick, first)[:1]
    gbmid_ref[...] = mm_nt(pick, last)[:1]


def like(shape, dtype):
    return jax.ShapeDtypeStruct(shape, dtype)


def sems(count):
    return [pltpu.SemaphoreType.DMA((count,)), pltpu.SemaphoreType.DMA((count,))]


def on_device(
    prognostic, cotangent, damping, in_scale, w_in, b_in, w_mid, b_mid, w_out, wave_order, lat_order
):
    high, low = dft_tables()
    order = wave_order.reshape(1, TRUNC)
    lats = lat_order.reshape(1, 256)
    count = ROWS * USED
    waves16 = pltpu.VMEM((N_LAT, PAD, 128), bf16)
    waves32 = pltpu.VMEM((N_LAT, PAD, 128), f32)
    blocks = pltpu.VMEM((N_LEV, PAD, NLON), bf16)
    wide16 = pltpu.VMEM((512, NLON), bf16)
    wide32 = pltpu.VMEM((512, NLON), f32)
    skinny = pltpu.VMEM((128, NLON), bf16)
    chunk = pltpu.VMEM((N_LEV, PAD, 256), bf16)
    widths = (256, 128)

    def per_unit(dtype, *leading):
        return [pltpu.VMEM((*leading, 16, width), dtype) for width in widths]

    spec_shape = like((WAVES, 2, 3, 4, TRUNC), f32)
    state_shape = like((count, NLON), f32)
    total_shapes = [like((2, N_LAT, 16, width), bf16) for width in widths]
    scratch = [
        pltpu.VMEM((count, NLON), f32), pltpu.VMEM((count, NLON), bf16),
        pltpu.VMEM((NLON, 512), bf16), pltpu.VMEM((NLON, 512), bf16),
        pltpu.VMEM((96, 512), bf16), pltpu.VMEM((512, 512), bf16), pltpu.VMEM((96, 512), bf16),
        pltpu.VMEM(spec_shape.shape, f32), pltpu.VMEM(state_shape.shape, f32),
        *per_unit(bf16, 2, N_LAT),
        pltpu.VMEM((TRUNC, TRUNC), bf16),
        pltpu.VMEM((WAVES, TRUNC, 256), bf16), pltpu.VMEM((WAVES, TRUNC, 256), bf16),
        pltpu.VMEM((NLON, 512), bf16), pltpu.VMEM((NLON, 512), bf16), pltpu.SemaphoreType.DMA((16,)),
        pltpu.VMEM((576, 128), f32), pltpu.VMEM((128, NLON), f32), waves32, blocks, blocks,
        waves16, waves16, pltpu.VMEM((2 * HALF, 128), f32), waves32, waves32,
        pltpu.VMEM((576, 128), f32), pltpu.VMEM((128, 512), bf16), pltpu.VMEM((128, 512), bf16),
        *[chunk] * 6,
        pltpu.VMEM((512, 128), bf16), pltpu.VMEM((128, 512), bf16), pltpu.VMEM((512, 128), bf16),
        pltpu.VMEM((512, 512), bf16), pltpu.VMEM((512, 128), f32), pltpu.VMEM((512, 128), f32),
        skinny, skinny, wide32, wide16, wide32, wide16, wide16, wide16,
        pltpu.VMEM((512, 128), f32), skinny, blocks, blocks,
        *per_unit(bf16, 2, N_LAT), *per_unit(bf16, N_LAT) * 3,
        *per_unit(f32), *per_unit(f32, 4), *per_unit(bf16),
    ]
    lat_sems, lev_sems, one_sems = sems(N_LAT), sems(N_LEV), sems(1)
    scratch += lat_sems + lev_sems + lat_sems + lev_sems * 3
    scratch += lev_sems + one_sems + lat_sems
    scratch += one_sems + lat_sems + lev_sems * 2 + lat_sems * 2 + one_sems * 2
    passed = pl.pallas_call(
        step_kernel,
        out_shape=[spec_shape, state_shape, *total_shapes],
        in_specs=[FAR] * 4 + [VMEM] * 3 + [SMEM] * 3 + [FAR, VMEM, FAR, VMEM, FAR],
        out_specs=[FAR] * 4,
        scratch_shapes=scratch,
        compiler_params=pltpu.CompilerParams(collective_id=0, has_side_effects=True),
        name="step",
    )(
        prognostic.reshape(count, NLON), cotangent.reshape(count, NLON), high, low, order, lats,
        diagonal_table(), degree_table(), damping, in_scale,
        w_in.T, b_in.reshape(1, 512), w_mid, b_mid.reshape(1, 512), w_out,
    )
    spectral, state, gin, gbin, gmid, gbmid, gout = pl.pallas_call(
        finish_kernel,
        out_shape=[
            spec_shape, state_shape,
            like((96, 512), f32), like((1, 512), f32), like((512, 512), f32), like((1, 512), f32),
            like((96, 512), f32),
        ],
        in_specs=[VMEM] * 4,
        out_specs=[VMEM] * 7,
        name="finish",
    )(*passed)
    spectral = jnp.swapaxes(spectral, 2, 3)
    return (
        state.reshape(prognostic.shape), spectral, gin.T, gbin.reshape(512), gmid, gbmid.reshape(512), gout,
    )


def solution(mesh):
    return jax.shard_map(
        on_device,
        mesh=mesh,
        in_specs=(
            P(None, "lev", "lat", None),
            P(None, "lev", "lat", None),
            P(None, "lev"),
            P(),
            P(),
            P(),
            P(),
            P(),
            P(),
            P(),
            P(),
        ),
        out_specs=(
            P(None, "lev", "lat", None),
            P("lat", None, None, "lev", None),
            P(),
            P(),
            P(),
            P(),
            P(),
        ),
        check_vma=False,
    )
```
